32 devices in a mesh: dom: 4 (over y, x), tp: 8 (over z, core).
Axes of the slice: x: 2, y: 2, z: 4, core: 2. Of those that a mesh axis runs over, the one named last changes fastest.
Arguments:
- latent: bfloat16 [1024, 16384], P('tp', 'dom'), may hold values from -6 to 6
- w_first: bfloat16 [1024, 1024], P(None, 'tp'), may hold values from -0.1875 to 0.1875
- w_second: bfloat16 [1024, 1024], P('tp'), may hold values from -0.1875 to 0.1875
- w_env: bfloat16 [1024, 256], P('tp'), may hold values from -0.1875 to 0.1875
- edge_vec: float32 [3, 16384], P(None, 'dom'), may hold values from -3 to 3, as said below
- centers: int32 [16384], P('dom'), may hold values from 0 to 127
- block_dest: int32 [128, 1], P('dom'), may hold values from 0 to 3; in each aligned block of 32 rows (0 to 31, 32 to 63, ...) at most 16 rows name the same one
- block_fill: int32 [128], P('dom'), may hold values from 64 to 128
- species: int32 [512], P('dom'), may hold values from 0 to 3
- species_gain: float32 [4, 256], P(None, 'tp'), may hold values from 0.1 to 1.9
Outputs:
- latent_new: bfloat16 [1024, 16384], P('tp', 'dom')
- env_out: float32 [9, 256, 512], P(None, 'tp', 'dom')
- invariants: float32 [3, 256, 16384], P(None, 'tp', 'dom')
The draws below stay inside these ranges and needn't reach their ends.
Inputs may be any that keep to these rules, and one draw needn't show every extreme that they name: `block_dest`: in the 32 blocks of one domain no destination domain is named more than 16 times, a bound that some block reaches. `edge_vec`: every component has magnitude 0.5 to 3.
All inputs are finite; a program needn't handle non-finite values.
Results may differ from the reference program's by a relative error of at most 0.0077.
Values may be sent and summed in bfloat16 or wider, within the bound.
No kernel may reach another device: no remote copies, remote signals or barrier semaphores. Data moves between devices by JAX's collectives and lax.ppermute only.
A program may use at most 128 MiB of HBM per device.

```python
import math
import jax
import jax.numpy as jnp
import numpy as np
from jax import lax

LAT = 1024
C = 256
NSPEC = 4
NBLK = 32
ATOM_DEV = 128
EDGES = 16384
N_ATOMS = 512
SLOTS = 16
N_DOM = 4


def draw_edge_vec(key, part):
    key_mag = jax.random.fold_in(key, 11)
    key_sign = jax.random.fold_in(key, 12)
    magnitude = jax.random.uniform(key_mag, (3, EDGES), jnp.float32, 0.5, 3.0)
    flips = jax.random.bernoulli(key_sign, 0.5, (3, EDGES))
    signed = jnp.where(flips, magnitude, -magnitude)
    return signed.astype(jnp.float32)


def set_ends(entries, own_key, low, largest):
    dims = entries.shape
    spot = [jax.random.randint(jax.random.fold_in(own_key, axis), (), 0, dims[axis]) for axis in range(len(dims))]
    entries = entries.at[tuple(spot)].set(low)
    longest = dims.index(max(dims))
    spot[longest] = (spot[longest] + 1) % dims[longest]
    return entries.at[tuple(spot)].set(largest)


def shard_levels(own_key, shape, split, smallest, largest):
    factor_of = 1.0
    for dim, shards_of in split:
        steps = jax.random.uniform(jax.random.fold_in(jax.random.fold_in(own_key, 6), dim), (shards_of,), jnp.float32, smallest / len(split), largest / len(split))
        factor_of = factor_of * jnp.repeat(jnp.exp(steps), shape[dim] // shards_of).reshape((-1,) + (1,) * (len(shape) - 1 - dim))
    return factor_of


def shared_out(rng, own, number, rows, number_of, top, bound, slope):
    sequence = jax.random.permutation(rng, number_of)
    heavy_load, ordinary = portions_of(number_of, rows * top, bound, slope, True), portions_of(number_of, rows * top, bound, slope, False)
    places = jnp.arange(number_of)

    def named(lengths, rotation):
        used = int((lengths > 0).sum())
        fixed = max(1, used // 4)
        shifted = fixed + (places - fixed + rotation * (used - fixed)) % max(1, number_of - fixed)
        return jnp.zeros((number_of,), jnp.int32).at[sequence[jnp.where(places < fixed, places, shifted)]].set(jnp.asarray(lengths, jnp.int32))

    lengths = jnp.where(number % 4 == 0, named(heavy_load, number // 4), named(ordinary, number - number // 4 - 1))
    mixed = jax.random.permutation(jax.random.fold_in(own, 3), number_of)
    donor, taker = mixed[0:number_of // 2 * 2:2], mixed[1:number_of // 2 * 2:2]
    room = jnp.minimum(lengths[donor] - 1, bound - lengths[taker]) // 2
    room = jnp.where((donor == sequence[0]) | (taker == sequence[0]) | (lengths[taker] == 0), 0, jnp.maximum(room, 0))
    shifted = jax.random.randint(jax.random.fold_in(own, 4), (number_of // 2,), 0, 1 << 20) % (room + 1)
    lengths = lengths.at[donor].add(-shifted).at[taker].add(shifted)
    labels = jnp.searchsorted(jnp.cumsum(lengths), jnp.arange(rows * top), side="right").astype(jnp.int32)
    listing = labels.reshape(top, rows).T
    listing = listing[jax.random.permutation(jax.random.fold_in(own, 1), rows)]
    rotation = jax.random.randint(jax.random.fold_in(own, 2), (rows, 1), 0, top)
    return jnp.take_along_axis(listing, (jnp.arange(top)[None, :] + rotation) % top, axis=1)


def portions_of(count, total, most, slope, full):
    portions = [(1 << 20) // math.isqrt(standing ** slope) + 1 for standing in range(1, count + 1)]
    largest = most if full else min(most, max(-(-total // count), total * portions[0] // sum(portions)))
    least = 1 if total - largest >= count - 1 else 0
    counts, spare = [largest] + [least] * (count - 1), total - largest - least * (count - 1)
    while spare > 0:
        free = [i for i in range(1, count) if counts[i] < largest] or [i for i in range(1, count) if counts[i] < most]
        mass, left = sum([portions[i] for i in free]), spare
        for i in free:
            more = min(most - counts[i], max(1, left * portions[i] // mass), spare)
            counts[i] = counts[i] + more
            spare = spare - more
    return np.array(counts)


def gaussian(rng, extent, spread, most, shards=(), held_as=jnp.bfloat16):
    entries = jax.random.normal(rng, extent, jnp.float32) * spread
    if len(shards) > 0:
        entries = shard_levels(rng, extent, shards, -0.22, 0.18) * entries
    return jnp.clip(entries, min=-most, max=most).astype(held_as)


def setup_inputs(seed: int = 0) -> dict:
    seeds = jax.random.split(jax.random.key(seed), 11)
    latent = gaussian(seeds[0], (LAT, EDGES), 1.0, 6.0, ((0, 8), (1, 4)))
    w_first = gaussian(seeds[1], (LAT, LAT), LAT ** -0.5, 0.1875, ((1, 8),))
    w_second = gaussian(seeds[2], (LAT, LAT), LAT ** -0.5, 0.1875, ((0, 8),))
    w_env = gaussian(seeds[3], (LAT, C), LAT ** -0.5, 0.1875, ((0, 8),))
    edge_vec = draw_edge_vec(jax.random.fold_in(seeds[10], 71), 0)
    centers = set_ends(jax.random.randint(seeds[5], (EDGES,), 0, ATOM_DEV), jax.random.fold_in(seeds[5], 1), 0, ATOM_DEV - 1).astype(jnp.int32)
    block_dest_keys = jax.random.split(jax.random.fold_in(seeds[6], 1), (N_DOM * NBLK) // NBLK)
    block_dest_turns = jax.random.permutation(jax.random.fold_in(seeds[6], 3), (N_DOM * NBLK) // NBLK)
    block_dest = jax.vmap(lambda own, number: shared_out(jax.random.fold_in(seeds[6], 2), own, number, NBLK, N_DOM, 1, SLOTS, 2))(block_dest_keys, block_dest_turns).reshape((N_DOM * NBLK, 1))
    block_fill = set_ends(jax.random.randint(seeds[7], (N_DOM * NBLK,), 64, 129), jax.random.fold_in(seeds[7], 1), 64, 128).astype(jnp.int32)
    species = set_ends(jax.random.randint(seeds[8], (N_ATOMS,), 0, NSPEC), jax.random.fold_in(seeds[8], 1), 0, NSPEC - 1).astype(jnp.int32)
    species_gain = jnp.clip(1.0 + 0.18 * jax.random.normal(seeds[9], (NSPEC, C), jnp.float32), 0.1, 1.9)
    return dict(latent=latent, w_first=w_first, w_second=w_second, w_env=w_env, edge_vec=edge_vec, centers=centers, block_dest=block_dest, block_fill=block_fill, species=species, species_gain=species_gain)


root_three = math.sqrt(3.0)
root_five = math.sqrt(5.0)
root_fifteen = math.sqrt(15.0)
cutoff_radius = 6.0
env_factor = 0.25

def harmonics(vectors):
    along_x = vectors[0]
    along_y = vectors[1]
    along_z = vectors[2]
    radius = jnp.sqrt(along_x * along_x + along_y * along_y + along_z * along_z)
    unit_x = along_x / radius
    unit_y = along_y / radius
    unit_z = along_z / radius
    ratio = radius / cutoff_radius
    envelope = (1.0 - ratio * ratio) ** 2
    parts = [jnp.ones_like(unit_x), root_three * unit_x, root_three * unit_y, root_three * unit_z, root_fifteen * unit_x * unit_y, root_fifteen * unit_y * unit_z, root_five / 2.0 * (3.0 * unit_z * unit_z - 1.0), root_fifteen * unit_x * unit_z, root_fifteen / 2.0 * (unit_x * unit_x - unit_y * unit_y)]
    return jnp.stack(parts) * envelope[None, :]

def reference(latent, w_first, w_second, w_env, edge_vec, centers, block_dest, block_fill, species, species_gain):
    hidden = jax.nn.silu(jnp.dot(w_first.T, latent, preferred_element_type=jnp.float32)).astype(jnp.bfloat16)
    update = jnp.dot(w_second.T, hidden, preferred_element_type=jnp.float32)
    latent_new = (latent.astype(jnp.float32) + update).astype(jnp.bfloat16)
    weights = jnp.dot(w_env.T, latent_new, preferred_element_type=jnp.float32).astype(jnp.bfloat16)
    weight_full = weights.astype(jnp.float32)
    harmonic = harmonics(edge_vec)
    edge_ids = jnp.arange(EDGES, dtype=jnp.int32)
    block_of = edge_ids // 128
    position = edge_ids % 128
    alive_mask = (position < block_fill[block_of]).astype(jnp.float32)
    atom = (block_dest[block_of, 0] * ATOM_DEV + centers).astype(jnp.int32)
    contrib = (harmonic[:, None, :] * weight_full[None, :, :] * alive_mask[None, None, :]).astype(jnp.bfloat16)
    flattened = contrib.reshape(9 * C, EDGES).T.astype(jnp.float32)
    summed = jax.ops.segment_sum(flattened, atom, num_segments=N_ATOMS)
    env_raw = summed.T.reshape(9, C, N_ATOMS)
    gain_sel = species_gain[species].T
    env_out = env_raw * gain_sel[None, :, :] * env_factor
    env_edge = env_out.astype(jnp.bfloat16)[:, :, atom].astype(jnp.float32)
    products = env_edge * harmonic[:, None, :]
    degree_sums = jnp.stack([products[0], lax.optimization_barrier(jnp.sum(products[1:4], axis=0)), lax.optimization_barrier(jnp.sum(products[4:9], axis=0))])
    invariants = degree_sums * weight_full[None, :, :] * alive_mask[None, None, :]
    return (latent_new, env_out, invariants)
```

```python
import functools
import math

import jax
import jax.numpy as jnp
from jax import lax
from jax.experimental import pallas as pl
from jax.experimental.pallas import tpu as pltpu
from jax.sharding import PartitionSpec as P

root_three = math.sqrt(3.0)
root_five = math.sqrt(5.0)
root_fifteen = math.sqrt(15.0)
cutoff_radius = 6.0
env_factor = 0.25
lanes = 128
cores = 2
bf16 = jnp.bfloat16
f32 = jnp.float32


in_vmem = pl.BlockSpec(memory_space=pltpu.VMEM)
in_smem = pl.BlockSpec(memory_space=pltpu.SMEM)


def harmonics(vectors):
    along_x = vectors[0]
    along_y = vectors[1]
    along_z = vectors[2]
    radius = jnp.sqrt(along_x * along_x + along_y * along_y + along_z * along_z)
    unit_x = along_x / radius
    unit_y = along_y / radius
    unit_z = along_z / radius
    ratio = radius / cutoff_radius
    envelope = (1.0 - ratio * ratio) ** 2
    parts = [
        jnp.ones_like(unit_x),
        root_three * unit_x,
        root_three * unit_y,
        root_three * unit_z,
        root_fifteen * unit_x * unit_y,
        root_fifteen * unit_y * unit_z,
        root_five / 2.0 * (3.0 * unit_z * unit_z - 1.0),
        root_fifteen * unit_x * unit_z,
        root_fifteen / 2.0 * (unit_x * unit_x - unit_y * unit_y),
    ]
    return jnp.stack(parts) * envelope[None, ...]


def contract_rows(left, right):
    return lax.dot_general(
        left, right, (((0,), (0,)), ((), ())), preferred_element_type=f32
    )


def swap_blocks(array, axis):
    return lax.all_to_all(array, axis, split_axis=0, concat_axis=0, tiled=True)


def flip_dom(array, mask):
    count = lax.axis_size("dom")
    return lax.ppermute(array, "dom", [(i, i ^ mask) for i in range(count)])


def shift_chips(array, step):
    count = lax.axis_size("tp")
    chips = count // cores
    pairs = [(t, (t // cores + step) % chips * cores + t % cores) for t in range(count)]
    return lax.ppermute(array, "tp", pairs)


def other_core(array):
    count = lax.axis_size("tp")
    return lax.ppermute(array, "tp", [(t, t ^ 1) for t in range(count)])


def prepare_kernel(me_ref, first_ref, second_ref, env_ref, full_ref, own_ref):
    quarters = full_ref.shape[0]
    width = first_ref.shape[0] // quarters
    chan = env_ref.shape[1] // quarters
    for q in range(quarters):
        row = 0
        for start in range(q * width, (q + 1) * width, lanes):
            full_ref[q, row : row + lanes, :] = first_ref[start : start + lanes, :].T
            row += lanes
        full_ref[q, row : row + width, :] = second_ref[:, q * width : (q + 1) * width].T
        row += width
        full_ref[q, row : row + chan, :] = env_ref[:, q * chan : (q + 1) * chan].T
    own_ref[...] = full_ref[me_ref[0]]


def mlp_kernel(me_ref, x_ref, *refs, quarters, chips, chan):
    groups = 2
    per_group = 1 + quarters
    sources = [refs[g * per_group : (g + 1) * per_group] for g in range(groups)]
    new_ref, out_ref, first, second, env, moved, hidden = refs[groups * per_group :]
    shards, depth, edges = x_ref.shape
    total = shards * depth
    width = total // quarters
    per_quarter = shards // quarters
    dom, chip, core = me_ref[0], me_ref[1], me_ref[2]
    for j in range(quarters):
        for i in range(per_quarter):
            start = j * width + i * depth
            moved[start : start + depth, :] = x_ref[(dom ^ j) * per_quarter + i]
    for k in range(chips):
        for g in range(groups):
            at = (k * groups + g) * depth
            for j in range(quarters):
                if k == 0:
                    block = sources[g][0].at[dom ^ j]
                else:
                    block = sources[g][1 + j].at[k - 1]
                for i in range(width // lanes):
                    place = j * width + i * lanes
                    first[at : at + depth, place : place + lanes] = block[
                        i * depth : (i + 1) * depth, :
                    ]
                row = width // lanes * depth
                place = pl.multiple_of((dom ^ j) * width, lanes)
                second[pl.ds(place, width), at : at + depth] = block[row : row + width, :]
                row += width
                place = pl.multiple_of((dom ^ j) * chan, chan)
                env[pl.ds(place, chan), at : at + depth] = block[row : row + chan, :]
    value = jnp.dot(first[...], moved[...], preferred_element_type=f32)
    hidden[...] = (value / (1.0 + jnp.exp(-value))).astype(bf16)
    update = jnp.dot(second[...], hidden[...], preferred_element_type=f32)
    for s in range(shards):
        rows = slice(s * depth, (s + 1) * depth)
        new_ref[s] = (x_ref[s].astype(f32) + update[rows, :]).astype(bf16)
    for k in range(chips):
        for g in range(groups):
            at = (k * groups + g) * depth
            source = lax.rem(chip + chips - k, chips) * cores + (core if g == 0 else 1 - core)
            moved[at : at + depth, :] = new_ref[source]
    rows = jnp.dot(env[...], moved[...], preferred_element_type=f32).astype(bf16)
    per = rows.shape[0] // shards
    for s in range(shards):
        out_ref[s] = rows[s * per : (s + 1) * per, :]


def spread_mlp(edge_rows, w_first, w_second, w_env):
    domains = lax.axis_size("dom")
    shards = lax.axis_size("tp")
    chips = shards // cores
    total = w_first.shape[0]
    depth = w_first.shape[1]
    channels = w_env.shape[1]
    width = total // domains
    chan = channels // domains
    rows = 2 * width + chan
    dom = lax.axis_index("dom").astype(jnp.int32)
    place = lax.axis_index("tp").astype(jnp.int32)
    full, own = pl.pallas_call(
        prepare_kernel,
        out_shape=(
            jax.ShapeDtypeStruct((domains, rows, depth), bf16),
            jax.ShapeDtypeStruct((rows, depth), bf16),
        ),
        in_specs=[in_smem, in_vmem, in_vmem, in_vmem],
        out_specs=(in_vmem, in_vmem),
        name="prepare",
    )(dom[None], w_first, w_second, w_env)
    arrived = jnp.stack([shift_chips(own, k) for k in range(1, chips)])
    plane = [arrived] + [flip_dom(arrived, j) for j in range(1, domains)]
    mine = [full] + plane
    others = [other_core(array) for array in mine]
    me = jnp.stack([dom, place // cores, place % cores])
    edges = edge_rows.shape[2]
    return pl.pallas_call(
        functools.partial(mlp_kernel, quarters=domains, chips=chips, chan=chan),
        out_shape=(
            jax.ShapeDtypeStruct((shards, depth, edges), bf16),
            jax.ShapeDtypeStruct((shards, channels // shards, edges), bf16),
        ),
        in_specs=[in_smem] + [in_vmem] * (1 + 2 * len(mine)),
        out_specs=(in_vmem, in_vmem),
        scratch_shapes=[
            pltpu.VMEM((total, total), bf16),
            pltpu.VMEM((total, total), bf16),
            pltpu.VMEM((channels, total), bf16),
            pltpu.VMEM((total, edges), bf16),
            pltpu.VMEM((total, edges), bf16),
        ],
        compiler_params=pltpu.CompilerParams(vmem_limit_bytes=60000 * 1024),
        name="mlp",
    )(me, edge_rows, *mine, *others)


def gathered_mlp(edge_rows, w_first, w_second, w_env):
    shards, depth, edges = edge_rows.shape
    flat = edge_rows.reshape(shards * depth, edges)
    full_first = lax.all_gather(w_first, "tp", axis=1, tiled=True)
    full_second = lax.all_gather(w_second, "tp", axis=0, tiled=True)
    full_env = lax.all_gather(w_env, "tp", axis=0, tiled=True)
    hidden = jax.nn.silu(contract_rows(full_first, flat)).astype(bf16)
    update = contract_rows(full_second, hidden)
    new_rows = (flat.astype(f32) + update).astype(bf16)
    weight_rows = contract_rows(full_env, new_rows).astype(bf16)
    return new_rows.reshape(shards, depth, edges), weight_rows.reshape(shards, -1, edges)


def select_atoms(centers_ref, block, atoms):
    ids = lax.broadcasted_iota(jnp.int32, (atoms, lanes), 0)
    return (ids == centers_ref[pl.ds(block, 1), :]).astype(f32).astype(bf16)


def sums_kernel(dest_ref, me_ref, w_ref, h_ref, centers_ref, *refs):
    outs, total = refs[:-1], refs[-1]
    shards, chan, edges = w_ref.shape
    atoms = total.shape[2]
    per = edges // lanes
    total[...] = jnp.zeros_like(total)

    def step(s, carry):
        for i in range(per):
            block = s * per + i
            weight = w_ref[s, :, i * lanes : (i + 1) * lanes].astype(f32)
            parts = [
                (h_ref[m, pl.ds(block, 1), :] * weight).astype(bf16)
                for m in range(h_ref.shape[0])
            ]
            contrib = jnp.concatenate(parts, axis=0)
            chosen = select_atoms(centers_ref, block, atoms)
            slot = dest_ref[block] ^ me_ref[0]
            total[slot] += lax.dot_general(
                contrib, chosen, (((1,), (1,)), ((), ())), preferred_element_type=f32
            )
        return carry

    lax.fori_loop(0, shards, step, 0)
    for j, out in enumerate(outs):
        out[...] = total[j].astype(out.dtype)


def invariants_kernel(dest_ref, me_ref, w_ref, h_ref, centers_ref, *refs):
    domains = len(refs) - 2
    out_ref, env = refs[domains:]
    shards, chan, edges = w_ref.shape
    atoms = env.shape[2]
    per = edges // lanes
    for j in range(domains):
        env[j] = refs[j][...]

    def step(s, carry):
        for i in range(per):
            block = s * per + i
            weight = w_ref[s, :, i * lanes : (i + 1) * lanes].astype(f32)
            chosen = select_atoms(centers_ref, block, atoms)
            slot = dest_ref[block] ^ me_ref[0]
            found = jnp.dot(env[slot], chosen, preferred_element_type=f32)
            products = [
                found[m * chan : (m + 1) * chan, :] * h_ref[m, pl.ds(block, 1), :]
                for m in range(h_ref.shape[0])
            ]
            at = pl.multiple_of(block * lanes, lanes)
            out_ref[0, :, pl.ds(at, lanes)] = products[0] * weight
            out_ref[1, :, pl.ds(at, lanes)] = sum(products[2:4], products[1]) * weight
            out_ref[2, :, pl.ds(at, lanes)] = sum(products[5:9], products[4]) * weight
        return carry

    lax.fori_loop(0, shards, step, 0)


def on_device(
    latent,
    w_first,
    w_second,
    w_env,
    edge_vec,
    centers,
    block_dest,
    block_fill,
    species,
    species_gain,
):
    domains = lax.axis_size("dom")
    shards = lax.axis_size("tp")
    nblocks = block_fill.shape[0]
    atoms = species.shape[0]
    chan = species_gain.shape[1]
    depth, edges = latent.shape
    me = lax.axis_index("dom").astype(jnp.int32)[None]
    spread = (
        depth == lanes
        and w_first.shape[0] % (domains * lanes) == 0
        and w_env.shape[1] % (domains * 16) == 0
        and shards % cores == 0
    )
    pieces = latent.reshape(depth, shards, edges // shards).transpose(1, 0, 2)
    edge_rows = swap_blocks(pieces, "tp")
    mlp = spread_mlp if spread else gathered_mlp
    new_rows, weight_rows = mlp(edge_rows, w_first, w_second, w_env)

    slot_pos = jnp.arange(lanes, dtype=jnp.int32)[None, :]
    alive_mask = (slot_pos < block_fill[:, None]).astype(f32)
    harmonic = harmonics(edge_vec.reshape(3, nblocks, lanes)) * alive_mask[None]
    center_blocks = centers.reshape(nblocks, lanes)
    target = block_dest[:, 0]
    species_ids = jnp.arange(species_gain.shape[0], dtype=jnp.int32)
    gain_sel = jnp.sum(
        jnp.where(
            species[None, None, :] == species_ids[:, None, None], species_gain[:, :, None], 0.0
        ),
        axis=0,
    )

    weights = swap_blocks(weight_rows, "tp")
    new_rows, weights = lax.optimization_barrier((new_rows, weights))
    latent_new = swap_blocks(new_rows, "tp").transpose(1, 0, 2).reshape(depth, edges)

    rows = 9 * chan
    sums = pl.pallas_call(
        sums_kernel,
        out_shape=[jax.ShapeDtypeStruct((rows, atoms), f32)]
        + [jax.ShapeDtypeStruct((rows, atoms), bf16)] * (domains - 1),
        in_specs=[in_smem, in_smem] + [in_vmem] * 3,
        out_specs=[in_vmem] * domains,
        scratch_shapes=[pltpu.VMEM((domains, rows, atoms), f32)],
        name="sums",
    )(target, me, weights, harmonic, center_blocks)
    env_raw = sums[0]
    for j in range(1, domains):
        env_raw = env_raw + flip_dom(sums[j], j).astype(f32)
    env_out = env_raw.reshape(9, chan, atoms) * gain_sel[None, :, :] * env_factor
    env_half = env_out.astype(bf16).reshape(rows, atoms)
    looked = [env_half] + [flip_dom(env_half, j) for j in range(1, domains)]
    invariants = pl.pallas_call(
        invariants_kernel,
        out_shape=jax.ShapeDtypeStruct((3, chan, edges), f32),
        in_specs=[in_smem, in_smem] + [in_vmem] * (3 + domains),
        out_specs=in_vmem,
        scratch_shapes=[pltpu.VMEM((domains, rows, atoms), bf16)],
        name="invariants",
    )(target, me, weights, harmonic, center_blocks, *looked)
    return (latent_new, env_out, invariants)


def solution(mesh):
    in_specs = (
        P("tp", "dom"),
        P(None, "tp"),
        P("tp", None),
        P("tp", None),
        P(None, "dom"),
        P("dom"),
        P("dom", None),
        P("dom"),
        P("dom"),
        P(None, "tp"),
    )
    out_specs = (P("tp", "dom"), P(None, "tp", "dom"), P(None, "tp", "dom"))
    return jax.shard_map(
        on_device, mesh=mesh, in_specs=in_specs, out_specs=out_specs, check_vma=False
    )
```

```python
import functools
import math

import jax
import jax.numpy as jnp
from jax import lax
from jax.experimental import pallas as pl
from jax.experimental.pallas import tpu as pltpu
from jax.sharding import PartitionSpec as P


root_three = math.sqrt(3.0)
root_five = math.sqrt(5.0)
root_fifteen = math.sqrt(15.0)
cutoff_radius = 6.0
env_factor = 0.25
lanes = 128
cores = 2
bf16 = jnp.bfloat16
f32 = jnp.float32


mib = 1024 * 1024
in_vmem = pl.BlockSpec(memory_space=pltpu.VMEM)
in_smem = pl.BlockSpec(memory_space=pltpu.SMEM)


def harmonics(vectors):
    along_x = vectors[0]
    along_y = vectors[1]
    along_z = vectors[2]
    radius = jnp.sqrt(along_x * along_x + along_y * along_y + along_z * along_z)
    unit_x = along_x / radius
    unit_y = along_y / radius
    unit_z = along_z / radius
    ratio = radius / cutoff_radius
    envelope = (1.0 - ratio * ratio) ** 2
    parts = [
        jnp.ones_like(unit_x),
        root_three * unit_x,
        root_three * unit_y,
        root_three * unit_z,
        root_fifteen * unit_x * unit_y,
        root_fifteen * unit_y * unit_z,
        root_five / 2.0 * (3.0 * unit_z * unit_z - 1.0),
        root_fifteen * unit_x * unit_z,
        root_fifteen / 2.0 * (unit_x * unit_x - unit_y * unit_y),
    ]
    return [part * envelope for part in parts]


def contract_rows(left, right):
    return lax.dot_general(
        left, right, (((0,), (0,)), ((), ())), preferred_element_type=f32
    )


def swap_blocks(array, axis):
    return lax.all_to_all(array, axis, split_axis=0, concat_axis=0, tiled=True)


def flip_dom(array, mask):
    count = lax.axis_size("dom")
    return lax.ppermute(array, "dom", [(i, i ^ mask) for i in range(count)])


def shift_chips(array, step):
    count = lax.axis_size("tp")
    chips = count // cores
    pairs = [(t, (t // cores + step) % chips * cores + t % cores) for t in range(count)]
    return lax.ppermute(array, "tp", pairs)


def flip_tp(array, mask):
    count = lax.axis_size("tp")
    return lax.ppermute(array, "tp", [(t, t ^ mask) for t in range(count)])


def other_core(array):
    return flip_tp(array, 1)


def prepare_kernel(me_ref, first_ref, second_ref, env_ref, full_ref, own_ref):
    quarters = full_ref.shape[0]
    width = first_ref.shape[0] // quarters
    chan = env_ref.shape[1] // quarters
    for q in range(quarters):
        row = 0
        for start in range(q * width, (q + 1) * width, lanes):
            full_ref[q, row : row + lanes, :] = first_ref[start : start + lanes, :].T
            row += lanes
        full_ref[q, row : row + width, :] = second_ref[:, q * width : (q + 1) * width].T
        row += width
        full_ref[q, row : row + chan, :] = env_ref[:, q * chan : (q + 1) * chan].T
    own_ref[...] = full_ref[me_ref[0]]


def mlp_kernel(me_ref, x_ref, *refs, quarters, chips, chan, batches):
    per_group = 1 + len(batches) * quarters
    sources = [refs[g * per_group : (g + 1) * per_group] for g in range(cores)]
    shards, depth, _ = x_ref.shape
    outs = refs[cores * per_group :]
    new_refs, (out_ref, first, second, env, moved, hidden, fresh) = outs[:shards], outs[shards:]
    total = shards * depth
    width = total // quarters
    per_quarter = shards // quarters
    dom, chip, core = me_ref[0], me_ref[1], me_ref[2]
    for j in range(quarters):
        for i in range(per_quarter):
            start = j * width + i * depth
            moved[start : start + depth, :] = x_ref[(dom ^ j) * per_quarter + i]
    order = [(0, None, 0)]
    for batch, steps in enumerate(batches):
        order += [(k, batch, at) for at, k in enumerate(steps)]
    for k, batch, within in order:
        for g in range(cores):
            at = (k * cores + g) * depth
            for j in range(quarters):
                if batch is None:
                    block = sources[g][0].at[dom ^ j]
                else:
                    block = sources[g][1 + batch * quarters + j].at[within]
                for i in range(width // lanes):
                    place = j * width + i * lanes
                    first[at : at + depth, place : place + lanes] = block[
                        i * depth : (i + 1) * depth, :
                    ]
                row = width // lanes * depth
                place = pl.multiple_of((dom ^ j) * width, lanes)
                second[pl.ds(place, width), at : at + depth] = block[row : row + width, :]
                row += width
                place = pl.multiple_of((dom ^ j) * chan, chan)
                env[pl.ds(place, chan), at : at + depth] = block[row : row + chan, :]
    value = jnp.dot(first[...], moved[...], preferred_element_type=f32)
    hidden[...] = (value / (1.0 + jnp.exp(-value))).astype(bf16)
    update = jnp.dot(second[...], hidden[...], preferred_element_type=f32)
    for s in range(shards):
        rows = slice(s * depth, (s + 1) * depth)
        fresh[s] = (x_ref[s].astype(f32) + update[rows, :]).astype(bf16)
    for s, out in enumerate(new_refs):
        out[...] = fresh[(chip * cores + core) ^ s]
    for k in range(chips):
        for g in range(cores):
            at = (k * cores + g) * depth
            source = lax.rem(chip + chips - k, chips) * cores + (core if g == 0 else 1 - core)
            moved[at : at + depth, :] = fresh[source]
    rows = jnp.dot(env[...], moved[...], preferred_element_type=f32).astype(bf16)
    per = rows.shape[0] // shards
    for s in range(shards):
        out_ref[s] = rows[s * per : (s + 1) * per, :]


def split_kernel(x_ref, tie_ref, out_ref):
    edges = out_ref.shape[2]
    for s in range(out_ref.shape[0]):
        out_ref[s] = x_ref[:, s * edges : (s + 1) * edges]


def join_kernel(me_ref, *refs):
    pieces, out_ref = refs[:-1], refs[-1]
    edges = pieces[0].shape[1]
    for s, piece in enumerate(pieces):
        at = pl.multiple_of((me_ref[0] ^ s) * edges, lanes)
        out_ref[:, pl.ds(at, edges)] = piece[...]


def spread_mlp(latent, w_first, w_second, w_env):
    domains = lax.axis_size("dom")
    shards = lax.axis_size("tp")
    chips = shards // cores
    total = w_first.shape[0]
    depth = w_first.shape[1]
    channels = w_env.shape[1]
    width = total // domains
    chan = channels // domains
    rows = 2 * width + chan
    edges = latent.shape[1] // shards
    dom = lax.axis_index("dom").astype(jnp.int32)
    place = lax.axis_index("tp").astype(jnp.int32)
    full, own = pl.pallas_call(
        prepare_kernel,
        out_shape=(
            jax.ShapeDtypeStruct((domains, rows, depth), bf16),
            jax.ShapeDtypeStruct((rows, depth), bf16),
        ),
        in_specs=[in_smem, in_vmem, in_vmem, in_vmem],
        out_specs=(in_vmem, in_vmem),
        compiler_params=pltpu.CompilerParams(vmem_limit_bytes=8 * mib),
        name="prepare",
    )(dom[None], w_first, w_second, w_env)
    pieces = pl.pallas_call(
        split_kernel,
        out_shape=jax.ShapeDtypeStruct((shards, depth, edges), bf16),
        in_specs=[in_vmem, pl.BlockSpec(memory_space=pl.ANY)],
        out_specs=in_vmem,
        compiler_params=pltpu.CompilerParams(vmem_limit_bytes=8 * mib),
        name="split",
    )(latent, own)
    shifted = {k: shift_chips(own, k) for k in range(1, chips)}
    edge_rows = swap_blocks(pieces, "tp")
    near = [k for k in (1, chips - 1)]
    batches = [near, [k for k in range(2, chips - 1)]]
    mine = [full]
    for steps in batches:
        arrived = jnp.stack([shifted[k] for k in steps])
        mine += [arrived] + [flip_dom(arrived, j) for j in range(1, domains)]
    others = [other_core(array) for array in mine]
    me = jnp.stack([dom, place // cores, place % cores])
    *new_rows, weight_rows = pl.pallas_call(
        functools.partial(mlp_kernel, quarters=domains, chips=chips, chan=chan, batches=batches),
        out_shape=[jax.ShapeDtypeStruct((depth, edges), bf16)] * shards
        + [jax.ShapeDtypeStruct((shards, channels // shards, edges), bf16)],
        in_specs=[in_smem] + [in_vmem] * (1 + 2 * len(mine)),
        out_specs=[in_vmem] * (shards + 1),
        scratch_shapes=[
            pltpu.VMEM((total, total), bf16),
            pltpu.VMEM((total, total), bf16),
            pltpu.VMEM((channels, total), bf16),
            pltpu.VMEM((total, edges), bf16),
            pltpu.VMEM((total, edges), bf16),
            pltpu.VMEM((shards, depth, edges), bf16),
        ],
        compiler_params=pltpu.CompilerParams(vmem_limit_bytes=28 * mib),
        name="mlp",
    )(me, edge_rows, *mine, *others)
    weights = swap_blocks(weight_rows, "tp")
    back = [new_rows[0]] + [flip_tp(new_rows[s], s) for s in range(1, shards)]
    latent_new = pl.pallas_call(
        join_kernel,
        out_shape=jax.ShapeDtypeStruct(latent.shape, bf16),
        in_specs=[in_smem] + [in_vmem] * shards,
        out_specs=in_vmem,
        compiler_params=pltpu.CompilerParams(vmem_limit_bytes=8 * mib),
        name="join",
    )(place[None], *back)
    return latent_new, weights


def gathered_mlp(latent, w_first, w_second, w_env):
    edge_rows = lax.all_to_all(latent, "tp", split_axis=1, concat_axis=0, tiled=True)
    full_first = lax.all_gather(w_first, "tp", axis=1, tiled=True)
    full_second = lax.all_gather(w_second, "tp", axis=0, tiled=True)
    full_env = lax.all_gather(w_env, "tp", axis=0, tiled=True)
    hidden = jax.nn.silu(contract_rows(full_first, edge_rows)).astype(bf16)
    update = contract_rows(full_second, hidden)
    new_rows = (edge_rows.astype(f32) + update).astype(bf16)
    weight_rows = contract_rows(full_env, new_rows).astype(bf16)
    shards = lax.axis_size("tp")
    weights = swap_blocks(weight_rows.reshape(shards, -1, weight_rows.shape[1]), "tp")
    new_rows, weights = lax.optimization_barrier((new_rows, weights))
    return lax.all_to_all(new_rows, "tp", split_axis=0, concat_axis=1, tiled=True), weights


def geometry_kernel(vec_ref, fill_ref, out_ref):
    vectors = [vec_ref[i] for i in range(3)]
    ids = lax.broadcasted_iota(jnp.int32, vectors[0].shape, 1)
    alive = (ids < fill_ref[...]).astype(f32)
    for m, part in enumerate(harmonics(vectors)):
        out_ref[m] = part * alive


def select_atoms(centers_ref, block, atoms):
    ids = lax.broadcasted_iota(jnp.int32, (atoms, lanes), 0)
    return (ids == centers_ref[pl.ds(block, 1), :]).astype(f32).astype(bf16)


def sums_kernel(dest_ref, me_ref, w_ref, h_ref, centers_ref, *refs):
    outs, total = refs[:-1], refs[-1]
    shards, _, edges = w_ref.shape
    atoms = total.shape[2]
    per = edges // lanes
    total[...] = jnp.zeros_like(total)

    def step(s, carry):
        for i in range(per):
            block = s * per + i
            weight = w_ref[s, :, i * lanes : (i + 1) * lanes].astype(f32)
            parts = [
                (h_ref[m, pl.ds(block, 1), :] * weight).astype(bf16)
                for m in range(h_ref.shape[0])
            ]
            contrib = jnp.concatenate(parts, axis=0)
            chosen = select_atoms(centers_ref, block, atoms)
            slot = dest_ref[block] ^ me_ref[0]
            total[slot] += lax.dot_general(
                contrib, chosen, (((1,), (1,)), ((), ())), preferred_element_type=f32
            )
        return carry

    lax.fori_loop(0, shards, step, 0)
    for j, out in enumerate(outs):
        out[...] = total[j].astype(out.dtype)


def invariants_kernel(dest_ref, me_ref, w_ref, h_ref, centers_ref, *refs):
    domains = len(refs) - 2
    out_ref, env = refs[domains:]
    shards, chan, edges = w_ref.shape
    atoms = env.shape[2]
    per = edges // lanes
    for j in range(domains):
        env[j] = refs[j][...]

    def step(s, carry):
        for i in range(per):
            block = s * per + i
            weight = w_ref[s, :, i * lanes : (i + 1) * lanes].astype(f32)
            chosen = select_atoms(centers_ref, block, atoms)
            slot = dest_ref[block] ^ me_ref[0]
            found = jnp.dot(env[slot], chosen, preferred_element_type=f32)
            products = [
                found[m * chan : (m + 1) * chan, :] * h_ref[m, pl.ds(block, 1), :]
                for m in range(h_ref.shape[0])
            ]
            at = pl.multiple_of(block * lanes, lanes)
            out_ref[0, :, pl.ds(at, lanes)] = products[0] * weight
            out_ref[1, :, pl.ds(at, lanes)] = sum(products[2:4], products[1]) * weight
            out_ref[2, :, pl.ds(at, lanes)] = sum(products[5:9], products[4]) * weight
        return carry

    lax.fori_loop(0, shards, step, 0)


def on_device(
    latent,
    w_first,
    w_second,
    w_env,
    edge_vec,
    centers,
    block_dest,
    block_fill,
    species,
    species_gain,
):
    domains = lax.axis_size("dom")
    shards = lax.axis_size("tp")
    nblocks = block_fill.shape[0]
    atoms = species.shape[0]
    chan = species_gain.shape[1]
    depth, edges = latent.shape
    me = lax.axis_index("dom").astype(jnp.int32)[None]
    spread = (
        depth == lanes
        and w_first.shape[0] % (domains * lanes) == 0
        and w_env.shape[1] % (domains * 16) == 0
        and shards % cores == 0
    )
    mlp = spread_mlp if spread else gathered_mlp
    latent_new, weights = mlp(latent, w_first, w_second, w_env)

    harmonic = pl.pallas_call(
        geometry_kernel,
        out_shape=jax.ShapeDtypeStruct((9, nblocks, lanes), f32),
        in_specs=[in_vmem, in_vmem],
        out_specs=in_vmem,
        compiler_params=pltpu.CompilerParams(vmem_limit_bytes=4 * mib),
        name="geometry",
    )(edge_vec.reshape(3, nblocks, lanes), block_fill[:, None])
    center_blocks = centers.reshape(nblocks, lanes)
    target = block_dest[:, 0]
    species_ids = jnp.arange(species_gain.shape[0], dtype=jnp.int32)
    gain_sel = jnp.sum(
        jnp.where(
            species[None, None, :] == species_ids[:, None, None], species_gain[:, :, None], 0.0
        ),
        axis=0,
    )

    rows = 9 * chan
    sums = pl.pallas_call(
        sums_kernel,
        out_shape=[jax.ShapeDtypeStruct((rows, atoms), f32)]
        + [jax.ShapeDtypeStruct((rows, atoms), bf16)] * (domains - 1),
        in_specs=[in_smem, in_smem] + [in_vmem] * 3,
        out_specs=[in_vmem] * domains,
        scratch_shapes=[pltpu.VMEM((domains, rows, atoms), f32)],
        compiler_params=pltpu.CompilerParams(vmem_limit_bytes=8 * mib),
        name="sums",
    )(target, me, weights, harmonic, center_blocks)
    env_raw = sums[0]
    for j in range(1, domains):
        env_raw = env_raw + flip_dom(sums[j], j).astype(f32)
    env_out = env_raw.reshape(9, chan, atoms) * gain_sel[None, :, :] * env_factor
    env_half = env_out.astype(bf16).reshape(rows, atoms)
    looked = [env_half] + [flip_dom(env_half, j) for j in range(1, domains)]
    invariants = pl.pallas_call(
        invariants_kernel,
        out_shape=jax.ShapeDtypeStruct((3, chan, edges), f32),
        in_specs=[in_smem, in_smem] + [in_vmem] * (3 + domains),
        out_specs=in_vmem,
        scratch_shapes=[pltpu.VMEM((domains, rows, atoms), bf16)],
        compiler_params=pltpu.CompilerParams(vmem_limit_bytes=10 * mib),
        name="invariants",
    )(target, me, weights, harmonic, center_blocks, *looked)
    return (latent_new, env_out, invariants)


def solution(mesh):
    in_specs = (
        P("tp", "dom"),
        P(None, "tp"),
        P("tp", None),
        P("tp", None),
        P(None, "dom"),
        P("dom"),
        P("dom", None),
        P("dom"),
        P("dom"),
        P(None, "tp"),
    )
    out_specs = (P("tp", "dom"), P(None, "tp", "dom"), P(None, "tp", "dom"))

    return jax.shard_map(on_device, mesh=mesh, in_specs=in_specs, out_specs=out_specs, check_vma=False)
```

```python
import functools
import math

import jax
import jax.numpy as jnp
from jax import lax
from jax.experimental import pallas as pl
from jax.experimental.pallas import tpu as pltpu
from jax.sharding import PartitionSpec as P


root_three = math.sqrt(3.0)
root_five = math.sqrt(5.0)
root_fifteen = math.sqrt(15.0)
cutoff_radius = 6.0
parts = 9
env_factor = 0.25
lanes = 128
cores = 2
bf16 = jnp.bfloat16
f32 = jnp.float32


mib = 1024 * 1024
in_vmem = pl.BlockSpec(memory_space=pltpu.VMEM)
in_smem = pl.BlockSpec(memory_space=pltpu.SMEM)
in_hbm = pl.BlockSpec(memory_space=pltpu.HBM)
anywhere = pl.BlockSpec(memory_space=pl.ANY)


def harmonics(vectors):
    along_x = vectors[0]
    along_y = vectors[1]
    along_z = vectors[2]
    radius = jnp.sqrt(along_x * along_x + along_y * along_y + along_z * along_z)
    unit_x = along_x / radius
    unit_y = along_y / radius
    unit_z = along_z / radius
    ratio = radius / cutoff_radius
    envelope = (1.0 - ratio * ratio) ** 2
    factors = [
        jnp.ones_like(unit_x),
        root_three * unit_x,
        root_three * unit_y,
        root_three * unit_z,
        root_fifteen * unit_x * unit_y,
        root_fifteen * unit_y * unit_z,
        root_five / 2.0 * (3.0 * unit_z * unit_z - 1.0),
        root_fifteen * unit_x * unit_z,
        root_fifteen / 2.0 * (unit_x * unit_x - unit_y * unit_y),
    ]
    return [factor * envelope for factor in factors]


def contract_rows(left, right):
    return lax.dot_general(
        left, right, (((0,), (0,)), ((), ())), preferred_element_type=f32
    )


def swap_blocks(array, axis):
    return lax.all_to_all(array, axis, split_axis=0, concat_axis=0, tiled=True)


def flip_dom(array, mask):
    count = lax.axis_size("dom")
    return lax.ppermute(array, "dom", [(i, i ^ mask) for i in range(count)])


def shift_chips(array, step):
    count = lax.axis_size("tp")
    chips = count // cores
    pairs = [(t, (t // cores + step) % chips * cores + t % cores) for t in range(count)]
    return lax.ppermute(array, "tp", pairs)


def flip_tp(array, mask):
    count = lax.axis_size("tp")
    return lax.ppermute(array, "tp", [(t, t ^ mask) for t in range(count)])


def other_core(array):
    return flip_tp(array, 1)


def stay(array):
    return pltpu.with_memory_space_constraint(array, pltpu.HBM)


def grant(size):
    return pltpu.CompilerParams(vmem_limit_bytes=size * mib)


def prepare_kernel(*refs):
    sources, (full_ref, own_ref), held, sems = refs[:3], refs[3:5], refs[5:8], refs[8]
    copies = [
        pltpu.make_async_copy(source, place, sems.at[i])
        for i, (source, place) in enumerate(zip(sources, held))
    ]
    for copy in copies:
        copy.start()
    first_ref, second_ref, env_ref = held
    quarters = full_ref.shape[0]
    width = first_ref.shape[0] // quarters
    chan = env_ref.shape[1] // quarters
    copies[0].wait()
    for q in range(quarters):
        for i in range(width // lanes):
            start = q * width + i * lanes
            full_ref[q, i * lanes : (i + 1) * lanes, :] = first_ref[start : start + lanes, :].T
    copies[1].wait()
    for q in range(quarters):
        full_ref[q, width : 2 * width, :] = second_ref[:, q * width : (q + 1) * width].T
    copies[2].wait()
    for q in range(quarters):
        full_ref[q, 2 * width :, :] = env_ref[:, q * chan : (q + 1) * chan].T
    own_ref[...] = full_ref[lax.axis_index("dom")]


def mlp_kernel(x_ref, *refs, quarters, chips, chan, batches):
    per_group = 1 + len(batches) * quarters
    sources = [refs[g * per_group : (g + 1) * per_group] for g in range(cores)]
    shards, depth, _ = x_ref.shape
    outs = refs[cores * per_group :]
    new_refs, outs = outs[:shards], outs[shards:]
    out_ref, first, second, env, moved, hidden, fresh, rows_out, sems = outs
    total = shards * depth
    width = total // quarters
    per_quarter = shards // quarters
    dom, place = lax.axis_index("dom"), lax.axis_index("tp")
    chip, core = place // cores, lax.rem(place, cores)
    for j in range(quarters):
        for i in range(per_quarter):
            start = j * width + i * depth
            moved[start : start + depth, :] = x_ref[(dom ^ j) * per_quarter + i]
    order = [(0, None, 0)]
    for batch, steps in enumerate(batches):
        order += [(k, batch, at) for at, k in enumerate(steps)]
    for k, batch, within in order:
        for g in range(cores):
            at = (k * cores + g) * depth
            for j in range(quarters):
                if batch is None:
                    block = sources[g][0].at[dom ^ j]
                else:
                    block = sources[g][1 + batch * quarters + j].at[within]
                for i in range(width // lanes):
                    column = j * width + i * lanes
                    first[at : at + depth, column : column + lanes] = block[
                        i * depth : (i + 1) * depth, :
                    ]
                row = width // lanes * depth
                start = pl.multiple_of((dom ^ j) * width, lanes)
                second[pl.ds(start, width), at : at + depth] = block[row : row + width, :]
                row += width
                start = pl.multiple_of((dom ^ j) * chan, chan)
                env[pl.ds(start, chan), at : at + depth] = block[row : row + chan, :]
    value = jnp.dot(first[...], moved[...], preferred_element_type=f32)
    hidden[...] = (value / (1.0 + jnp.exp(-value))).astype(bf16)
    update = jnp.dot(second[...], hidden[...], preferred_element_type=f32)
    for s in range(shards):
        rows = slice(s * depth, (s + 1) * depth)
        fresh[s] = (x_ref[s].astype(f32) + update[rows, :]).astype(bf16)
    copies = [
        pltpu.make_async_copy(fresh.at[place ^ s], out, sems.at[s])
        for s, out in enumerate(new_refs)
    ]
    for copy in copies:
        copy.start()
    for k in range(chips):
        for g in range(cores):
            at = (k * cores + g) * depth
            source = lax.rem(chip + chips - k, chips) * cores + (core if g == 0 else 1 - core)
            moved[at : at + depth, :] = fresh[source]
    rows = jnp.dot(env[...], moved[...], preferred_element_type=f32).astype(bf16)
    per = rows.shape[0] // shards
    for s in range(shards):
        rows_out[s] = rows[s * per : (s + 1) * per, :]
    copies.append(pltpu.make_async_copy(rows_out, out_ref, sems.at[shards]))
    copies[-1].start()
    for copy in copies:
        copy.wait()


def split_kernel(x_ref, tie_ref, out_ref, held, sems_in, sems_out):
    shards, _, edges = held.shape
    arriving = [
        pltpu.make_async_copy(x_ref.at[:, pl.ds(s * edges, edges)], held.at[s], sems_in.at[s])
        for s in range(shards)
    ]
    leaving = [
        pltpu.make_async_copy(held.at[s], out_ref.at[s], sems_out.at[s]) for s in range(shards)
    ]
    for copy in arriving:
        copy.start()
    for before, after in zip(arriving, leaving):
        before.wait()
        after.start()
    for copy in leaving:
        copy.wait()


def join_kernel(tie_ref, *refs):
    pieces, out_ref = refs[:-1], refs[-1]
    edges = pieces[0].shape[1]
    for s, piece in enumerate(pieces):
        at = pl.multiple_of((lax.axis_index("tp") ^ s) * edges, lanes)
        out_ref[:, pl.ds(at, edges)] = piece[...]


def join_pieces(back, tie):
    depth, edges = back[0].shape
    return pl.pallas_call(
        join_kernel,
        out_shape=jax.ShapeDtypeStruct((depth, edges * len(back)), bf16),
        in_specs=[anywhere] + [in_vmem] * len(back),
        out_specs=in_vmem,
        compiler_params=grant(8),
        name="join",
    )(tie, *back)


def spread_mlp(latent, w_first, w_second, w_env, ties):
    domains = lax.axis_size("dom")
    shards = lax.axis_size("tp")
    chips = shards // cores
    total = w_first.shape[0]
    depth = w_first.shape[1]
    channels = w_env.shape[1]
    width = total // domains
    chan = channels // domains
    rows = 2 * width + chan
    edges = latent.shape[1] // shards
    full, own = pl.pallas_call(
        prepare_kernel,
        out_shape=(
            jax.ShapeDtypeStruct((domains, rows, depth), bf16),
            jax.ShapeDtypeStruct((rows, depth), bf16),
        ),
        in_specs=[in_hbm] * 3,
        out_specs=(in_vmem, in_vmem),
        scratch_shapes=[pltpu.VMEM(w.shape, bf16) for w in (w_first, w_second, w_env)]
        + [pltpu.SemaphoreType.DMA((3,))],
        compiler_params=grant(8),
        name="prepare",
    )(stay(w_first), stay(w_second), stay(w_env))
    pieces = pl.pallas_call(
        split_kernel,
        out_shape=pltpu.HBM((shards, depth, edges), bf16),
        in_specs=[in_hbm, anywhere],
        out_specs=in_hbm,
        scratch_shapes=[pltpu.VMEM((shards, depth, edges), bf16)]
        + [pltpu.SemaphoreType.DMA((shards,))] * 2,
        compiler_params=grant(8),
        name="split",
    )(stay(latent), own)
    shifted = {k: shift_chips(own, k) for k in range(1, chips)}
    edge_rows = swap_blocks(pieces, "tp")
    edge_rows, *ties = lax.optimization_barrier((edge_rows, *ties))
    near = [k for k in (1, chips - 1)]
    batches = [near, [k for k in range(2, chips - 1)]]
    mine = [full]
    for steps in batches:
        arrived = jnp.stack([shifted[k] for k in steps])
        mine += [arrived] + [flip_dom(arrived, j) for j in range(1, domains)]
    others = [other_core(array) for array in mine]
    *new_rows, weight_rows = pl.pallas_call(
        functools.partial(mlp_kernel, quarters=domains, chips=chips, chan=chan, batches=batches),
        out_shape=[pltpu.HBM((depth, edges), bf16)] * shards
        + [pltpu.HBM((shards, channels // shards, edges), bf16)],
        in_specs=[in_vmem] * (1 + 2 * len(mine)),
        out_specs=[in_hbm] * (shards + 1),
        scratch_shapes=[
            pltpu.VMEM((total, total), bf16),
            pltpu.VMEM((total, total), bf16),
            pltpu.VMEM((channels, total), bf16),
            pltpu.VMEM((total, edges), bf16),
            pltpu.VMEM((total, edges), bf16),
            pltpu.VMEM((shards, depth, edges), bf16),
            pltpu.VMEM((shards, channels // shards, edges), bf16),
            pltpu.SemaphoreType.DMA((shards + 1,)),
        ],
        compiler_params=grant(28),
        name="mlp",
    )(edge_rows, *mine, *others)
    weights = swap_blocks(weight_rows, "tp")
    back = [new_rows[0]] + [flip_tp(new_rows[s], s) for s in range(1, shards)]
    return (lambda tie: join_pieces(back, tie)), weights, ties


def gathered_mlp(latent, w_first, w_second, w_env, ties):
    edge_rows = lax.all_to_all(latent, "tp", split_axis=1, concat_axis=0, tiled=True)
    full_first = lax.all_gather(w_first, "tp", axis=1, tiled=True)
    full_second = lax.all_gather(w_second, "tp", axis=0, tiled=True)
    full_env = lax.all_gather(w_env, "tp", axis=0, tiled=True)
    hidden = jax.nn.silu(contract_rows(full_first, edge_rows)).astype(bf16)
    update = contract_rows(full_second, hidden)
    new_rows = (edge_rows.astype(f32) + update).astype(bf16)
    weight_rows = contract_rows(full_env, new_rows).astype(bf16)
    shards = lax.axis_size("tp")
    weights = swap_blocks(weight_rows.reshape(shards, -1, weight_rows.shape[1]), "tp")
    new_rows, weights = lax.optimization_barrier((new_rows, weights))
    latent_new = lax.all_to_all(new_rows, "tp", split_axis=0, concat_axis=1, tiled=True)
    return (lambda tie: latent_new), weights, ties


def geometry_kernel(vec_ref, fill_ref, centers_ref, out_ref):
    vectors = [vec_ref[i] for i in range(3)]
    ids = lax.broadcasted_iota(jnp.int32, vectors[0].shape, 1)
    alive = (ids < fill_ref[...]).astype(f32)
    for m, part in enumerate(harmonics(vectors)):
        out_ref[m] = part * alive
    out_ref[parts] = centers_ref[...].astype(f32)


def select_atoms(h_ref, block, atoms):
    ids = lax.broadcasted_iota(jnp.int32, (atoms, lanes), 0).astype(f32)
    return (ids == h_ref[parts, pl.ds(block, 1), :]).astype(f32).astype(bf16)


def sums_kernel(dest_ref, w_ref, h_ref, *refs):
    outs, total = refs[:-1], refs[-1]
    shards, _, edges = w_ref.shape
    atoms = total.shape[2]
    per = edges // lanes
    total[...] = jnp.zeros_like(total)

    def step(s, carry):
        for i in range(per):
            block = s * per + i
            weight = w_ref[s, :, i * lanes : (i + 1) * lanes].astype(f32)
            terms = [
                (h_ref[m, pl.ds(block, 1), :] * weight).astype(bf16) for m in range(parts)
            ]
            contrib = jnp.concatenate(terms, axis=0)
            chosen = select_atoms(h_ref, block, atoms)
            slot = dest_ref[block] ^ lax.axis_index("dom")
            total[slot] += lax.dot_general(
                contrib, chosen, (((1,), (1,)), ((), ())), preferred_element_type=f32
            )
        return carry

    lax.fori_loop(0, shards, step, 0)
    for j, out in enumerate(outs):
        out[...] = total[j].astype(out.dtype)


def invariants_kernel(dest_ref, w_ref, h_ref, *refs):
    domains = len(refs) - 3
    out_ref, token_ref, env = refs[domains:]
    token_ref[...] = jnp.zeros_like(token_ref)
    shards, chan, edges = w_ref.shape
    atoms = env.shape[2]
    per = edges // lanes
    for j in range(domains):
        env[j] = refs[j][...]

    def step(s, carry):
        for i in range(per):
            block = s * per + i
            weight = w_ref[s, :, i * lanes : (i + 1) * lanes].astype(f32)
            chosen = select_atoms(h_ref, block, atoms)
            slot = dest_ref[block] ^ lax.axis_index("dom")
            found = jnp.dot(env[slot], chosen, preferred_element_type=f32)
            products = [
                found[m * chan : (m + 1) * chan, :] * h_ref[m, pl.ds(block, 1), :]
                for m in range(parts)
            ]
            at = pl.multiple_of(block * lanes, lanes)
            out_ref[0, :, pl.ds(at, lanes)] = products[0] * weight
            out_ref[1, :, pl.ds(at, lanes)] = sum(products[2:4], products[1]) * weight
            out_ref[2, :, pl.ds(at, lanes)] = sum(products[5:9], products[4]) * weight
        return carry

    lax.fori_loop(0, shards, step, 0)


def on_device(
    latent,
    w_first,
    w_second,
    w_env,
    edge_vec,
    centers,
    block_dest,
    block_fill,
    species,
    species_gain,
):
    domains = lax.axis_size("dom")
    shards = lax.axis_size("tp")
    nblocks = block_fill.shape[0]
    atoms = species.shape[0]
    chan = species_gain.shape[1]
    depth, edges = latent.shape
    spread = (
        depth == lanes
        and w_first.shape[0] % (domains * lanes) == 0
        and w_env.shape[1] % (domains * 16) == 0
        and shards % cores == 0
        and shards // cores >= 4
    )
    harmonic = pl.pallas_call(
        geometry_kernel,
        out_shape=jax.ShapeDtypeStruct((parts + 1, nblocks, lanes), f32),
        in_specs=[in_vmem] * 3,
        out_specs=in_vmem,
        compiler_params=grant(4),
        name="geometry",
    )(edge_vec.reshape(3, nblocks, lanes), block_fill[:, None], centers.reshape(nblocks, lanes))
    target = stay(block_dest[:, 0])
    species_ids = jnp.arange(species_gain.shape[0], dtype=jnp.int32)
    gain_sel = jnp.sum(
        jnp.where(
            species[None, None, :] == species_ids[:, None, None], species_gain[:, :, None], 0.0
        ),
        axis=0,
    )
    mlp = spread_mlp if spread else gathered_mlp
    finish, weights, (harmonic, gain_sel) = mlp(
        latent, w_first, w_second, w_env, (harmonic, gain_sel)
    )

    rows = parts * chan
    sums = pl.pallas_call(
        sums_kernel,
        out_shape=[jax.ShapeDtypeStruct((rows, atoms), f32)]
        + [jax.ShapeDtypeStruct((rows, atoms), bf16)] * (domains - 1),
        in_specs=[in_smem] + [in_vmem] * 2,
        out_specs=[in_vmem] * domains,
        scratch_shapes=[pltpu.VMEM((domains, rows, atoms), f32)],
        compiler_params=grant(8),
        name="sums",
    )(target, weights, harmonic)
    env_raw = sums[0]
    for j in range(1, domains):
        env_raw = env_raw + flip_dom(sums[j], j).astype(f32)
    env_out = env_raw.reshape(parts, chan, atoms) * gain_sel[None, :, :] * env_factor
    env_half = env_out.astype(bf16).reshape(rows, atoms)
    looked = [env_half] + [flip_dom(env_half, j) for j in range(1, domains)]
    invariants, token = pl.pallas_call(
        invariants_kernel,
        out_shape=(
            jax.ShapeDtypeStruct((3, chan, edges), f32),
            jax.ShapeDtypeStruct((8, lanes), f32),
        ),
        in_specs=[in_smem] + [in_vmem] * (2 + domains),
        out_specs=(in_vmem, in_vmem),
        scratch_shapes=[pltpu.VMEM((domains, rows, atoms), bf16)],
        compiler_params=grant(10),
        name="invariants",
    )(target, weights, harmonic, *looked)
    return (finish(token), env_out, invariants)


def solution(mesh):
    in_specs = (
        P("tp", "dom"),
        P(None, "tp"),
        P("tp", None),
        P("tp", None),
        P(None, "dom"),
        P("dom"),
        P("dom", None),
        P("dom"),
        P("dom"),
        P(None, "tp"),
    )
    out_specs = (P("tp", "dom"), P(None, "tp", "dom"), P(None, "tp", "dom"))

    return jax.shard_map(on_device, mesh=mesh, in_specs=in_specs, out_specs=out_specs, check_vma=False)
```

```python
import functools
import math

import jax
import jax.numpy as jnp
from jax import lax
from jax.experimental import pallas as pl
from jax.experimental.pallas import tpu as pltpu
from jax.sharding import PartitionSpec as P


root_three = math.sqrt(3.0)
root_five = math.sqrt(5.0)
root_fifteen = math.sqrt(15.0)
cutoff_radius = 6.0
parts = 9
env_factor = 0.25
lanes = 128
cores = 2
bf16 = jnp.bfloat16
f32 = jnp.float32


mib = 1024 * 1024
in_vmem = pl.BlockSpec(memory_space=pltpu.VMEM)
in_smem = pl.BlockSpec(memory_space=pltpu.SMEM)
in_hbm = pl.BlockSpec(memory_space=pltpu.HBM)
anywhere = pl.BlockSpec(memory_space=pl.ANY)


def harmonics(vectors):
    along_x = vectors[0]
    along_y = vectors[1]
    along_z = vectors[2]
    radius = jnp.sqrt(along_x * along_x + along_y * along_y + along_z * along_z)
    unit_x = along_x / radius
    unit_y = along_y / radius
    unit_z = along_z / radius
    ratio = radius / cutoff_radius
    envelope = (1.0 - ratio * ratio) ** 2
    factors = [
        jnp.ones_like(unit_x),
        root_three * unit_x,
        root_three * unit_y,
        root_three * unit_z,
        root_fifteen * unit_x * unit_y,
        root_fifteen * unit_y * unit_z,
        root_five / 2.0 * (3.0 * unit_z * unit_z - 1.0),
        root_fifteen * unit_x * unit_z,
        root_fifteen / 2.0 * (unit_x * unit_x - unit_y * unit_y),
    ]
    return [factor * envelope for factor in factors]


def contract_rows(left, right):
    return lax.dot_general(
        left, right, (((0,), (0,)), ((), ())), preferred_element_type=f32
    )


def swap_blocks(array, axis):
    return lax.all_to_all(array, axis, split_axis=0, concat_axis=0, tiled=True)


def flip_dom(array, mask):
    count = lax.axis_size("dom")
    return lax.ppermute(array, "dom", [(i, i ^ mask) for i in range(count)])


def hop_order(chips):
    return sorted(range(1, chips), key=lambda k: (k.bit_length(), -k))


def flip_tp(array, mask):
    count = lax.axis_size("tp")
    return lax.ppermute(array, "tp", [(t, t ^ mask) for t in range(count)])


def other_core(array):
    return flip_tp(array, 1)


def stay(array):
    return pltpu.with_memory_space_constraint(array, pltpu.HBM)


def grant(size):
    return pltpu.CompilerParams(vmem_limit_bytes=size * mib)


def prepare_kernel(*refs):
    sources, (full_ref, own_ref), held, sems = refs[:3], refs[3:5], refs[5:8], refs[8]
    copies = [
        pltpu.make_async_copy(source, place, sems.at[i])
        for i, (source, place) in enumerate(zip(sources, held))
    ]
    for copy in copies:
        copy.start()
    first_ref, second_ref, env_ref = held
    quarters = full_ref.shape[0]
    width = first_ref.shape[0] // quarters
    chan = env_ref.shape[1] // quarters
    copies[0].wait()
    for q in range(quarters):
        for i in range(width // lanes):
            start = q * width + i * lanes
            full_ref[q, i * lanes : (i + 1) * lanes, :] = first_ref[start : start + lanes, :].T
    copies[1].wait()
    for q in range(quarters):
        full_ref[q, width : 2 * width, :] = second_ref[:, q * width : (q + 1) * width].T
    copies[2].wait()
    for q in range(quarters):
        full_ref[q, 2 * width :, :] = env_ref[:, q * chan : (q + 1) * chan].T
    own_ref[...] = full_ref[lax.axis_index("dom")]


def mlp_kernel(x_ref, *refs, quarters, chips, chan, order):
    per_group = 1 + len(order) * quarters
    sources = [refs[g * per_group : (g + 1) * per_group] for g in range(cores)]
    shards, depth, _ = x_ref.shape
    outs = refs[cores * per_group :]
    new_refs, outs = outs[:shards], outs[shards:]
    out_ref, first, second, env, moved, hidden, fresh, rows_out, sems = outs
    total = shards * depth
    width = total // quarters
    per_quarter = shards // quarters
    dom, place = lax.axis_index("dom"), lax.axis_index("tp")
    chip, core = place // cores, lax.rem(place, cores)
    for j in range(quarters):
        for i in range(per_quarter):
            start = j * width + i * depth
            moved[start : start + depth, :] = x_ref[(dom ^ j) * per_quarter + i]
    for k in range(chips):
        for g in range(cores):
            at = (k * cores + g) * depth
            for j in range(quarters):
                if k == 0:
                    block = sources[g][0].at[dom ^ j]
                else:
                    block = sources[g][1 + order.index(k) * quarters + j]
                for i in range(width // lanes):
                    column = j * width + i * lanes
                    first[at : at + depth, column : column + lanes] = block[
                        i * depth : (i + 1) * depth, :
                    ]
                row = width // lanes * depth
                start = pl.multiple_of((dom ^ j) * width, lanes)
                second[pl.ds(start, width), at : at + depth] = block[row : row + width, :]
                row += width
                start = pl.multiple_of((dom ^ j) * chan, chan)
                env[pl.ds(start, chan), at : at + depth] = block[row : row + chan, :]
    value = jnp.dot(first[...], moved[...], preferred_element_type=f32)
    hidden[...] = (value / (1.0 + jnp.exp(-value))).astype(bf16)
    update = jnp.dot(second[...], hidden[...], preferred_element_type=f32)
    for s in range(shards):
        rows = slice(s * depth, (s + 1) * depth)
        fresh[s] = (x_ref[s].astype(f32) + update[rows, :]).astype(bf16)
    copies = [
        pltpu.make_async_copy(fresh.at[place ^ s], out, sems.at[s])
        for s, out in enumerate(new_refs)
    ]
    for copy in copies:
        copy.start()
    for k in range(chips):
        for g in range(cores):
            at = (k * cores + g) * depth
            source = (chip ^ k) * cores + (core if g == 0 else 1 - core)
            moved[at : at + depth, :] = fresh[source]
    rows = jnp.dot(env[...], moved[...], preferred_element_type=f32).astype(bf16)
    per = rows.shape[0] // shards
    for s in range(shards):
        rows_out[s] = rows[s * per : (s + 1) * per, :]
    copies.append(pltpu.make_async_copy(rows_out, out_ref, sems.at[shards]))
    copies[-1].start()
    for copy in copies:
        copy.wait()


def split_kernel(x_ref, tie_ref, out_ref, held, sems_in, sems_out):
    shards, _, edges = held.shape
    arriving = [
        pltpu.make_async_copy(x_ref.at[:, pl.ds(s * edges, edges)], held.at[s], sems_in.at[s])
        for s in range(shards)
    ]
    leaving = [
        pltpu.make_async_copy(held.at[s], out_ref.at[s], sems_out.at[s]) for s in range(shards)
    ]
    for copy in arriving:
        copy.start()
    for before, after in zip(arriving, leaving):
        before.wait()
        after.start()
    for copy in leaving:
        copy.wait()


def join_kernel(tie_ref, *refs):
    pieces, out_ref = refs[:-1], refs[-1]
    edges = pieces[0].shape[1]
    for s, piece in enumerate(pieces):
        at = pl.multiple_of((lax.axis_index("tp") ^ s) * edges, lanes)
        out_ref[:, pl.ds(at, edges)] = piece[...]


def join_pieces(back, tie):
    depth, edges = back[0].shape
    return pl.pallas_call(
        join_kernel,
        out_shape=jax.ShapeDtypeStruct((depth, edges * len(back)), bf16),
        in_specs=[anywhere] + [in_vmem] * len(back),
        out_specs=in_vmem,
        compiler_params=grant(8),
        name="join",
    )(tie, *back)


def spread_mlp(latent, w_first, w_second, w_env, ties):
    domains = lax.axis_size("dom")
    shards = lax.axis_size("tp")
    chips = shards // cores
    total = w_first.shape[0]
    depth = w_first.shape[1]
    channels = w_env.shape[1]
    width = total // domains
    chan = channels // domains
    rows = 2 * width + chan
    edges = latent.shape[1] // shards
    full, own = pl.pallas_call(
        prepare_kernel,
        out_shape=(
            jax.ShapeDtypeStruct((domains, rows, depth), bf16),
            jax.ShapeDtypeStruct((rows, depth), bf16),
        ),
        in_specs=[in_hbm] * 3,
        out_specs=(in_vmem, in_vmem),
        scratch_shapes=[pltpu.VMEM(w.shape, bf16) for w in (w_first, w_second, w_env)]
        + [pltpu.SemaphoreType.DMA((3,))],
        compiler_params=grant(8),
        name="prepare",
    )(stay(w_first), stay(w_second), stay(w_env))
    pieces = pl.pallas_call(
        split_kernel,
        out_shape=pltpu.HBM((shards, depth, edges), bf16),
        in_specs=[in_hbm, anywhere],
        out_specs=in_hbm,
        scratch_shapes=[pltpu.VMEM((shards, depth, edges), bf16)]
        + [pltpu.SemaphoreType.DMA((shards,))] * 2,
        compiler_params=grant(8),
        name="split",
    )(stay(latent), own)
    order = hop_order(chips)
    shifted = {}
    for k in order:
        shifted[k] = flip_tp(own, k * cores)
    edge_rows = swap_blocks(pieces, "tp")
    edge_rows, *ties = lax.optimization_barrier((edge_rows, *ties))
    mine = [full]
    for k in order:
        mine += [shifted[k]] + [flip_dom(shifted[k], j) for j in range(1, domains)]
    others = [other_core(array) for array in mine]
    *new_rows, weight_rows = pl.pallas_call(
        functools.partial(mlp_kernel, quarters=domains, chips=chips, chan=chan, order=order),
        out_shape=[pltpu.HBM((depth, edges), bf16)] * shards
        + [pltpu.HBM((shards, channels // shards, edges), bf16)],
        in_specs=[in_vmem] * (1 + 2 * len(mine)),
        out_specs=[in_hbm] * (shards + 1),
        scratch_shapes=[
            pltpu.VMEM((total, total), bf16),
            pltpu.VMEM((total, total), bf16),
            pltpu.VMEM((channels, total), bf16),
            pltpu.VMEM((total, edges), bf16),
            pltpu.VMEM((total, edges), bf16),
            pltpu.VMEM((shards, depth, edges), bf16),
            pltpu.VMEM((shards, channels // shards, edges), bf16),
            pltpu.SemaphoreType.DMA((shards + 1,)),
        ],
        compiler_params=grant(28),
        name="mlp",
    )(edge_rows, *mine, *others)
    weights = swap_blocks(weight_rows, "tp")
    back = {0: new_rows[0]}
    for s in range(1, shards):
        back[s] = flip_tp(new_rows[s], s)
    back = [back[s] for s in range(shards)]
    return (lambda tie: join_pieces(back, tie)), weights, ties


def gathered_mlp(latent, w_first, w_second, w_env, ties):
    edge_rows = lax.all_to_all(latent, "tp", split_axis=1, concat_axis=0, tiled=True)
    full_first = lax.all_gather(w_first, "tp", axis=1, tiled=True)
    full_second = lax.all_gather(w_second, "tp", axis=0, tiled=True)
    full_env = lax.all_gather(w_env, "tp", axis=0, tiled=True)
    hidden = jax.nn.silu(contract_rows(full_first, edge_rows)).astype(bf16)
    update = contract_rows(full_second, hidden)
    new_rows = (edge_rows.astype(f32) + update).astype(bf16)
    weight_rows = contract_rows(full_env, new_rows).astype(bf16)
    shards = lax.axis_size("tp")
    weights = swap_blocks(weight_rows.reshape(shards, -1, weight_rows.shape[1]), "tp")
    new_rows, weights = lax.optimization_barrier((new_rows, weights))
    latent_new = lax.all_to_all(new_rows, "tp", split_axis=0, concat_axis=1, tiled=True)
    return (lambda tie: latent_new), weights, ties


def geometry_kernel(vec_ref, fill_ref, centers_ref, out_ref):
    vectors = [vec_ref[i] for i in range(3)]
    ids = lax.broadcasted_iota(jnp.int32, vectors[0].shape, 1)
    alive = (ids < fill_ref[...]).astype(f32)
    for m, part in enumerate(harmonics(vectors)):
        out_ref[m] = part * alive
    out_ref[parts] = centers_ref[...].astype(f32)


def select_atoms(h_ref, block, atoms):
    ids = lax.broadcasted_iota(jnp.int32, (atoms, lanes), 0).astype(f32)
    return (ids == h_ref[parts, pl.ds(block, 1), :]).astype(f32).astype(bf16)


def sums_kernel(dest_ref, w_ref, h_ref, *refs):
    outs, total = refs[:-1], refs[-1]
    shards, _, edges = w_ref.shape
    atoms = total.shape[2]
    per = edges // lanes
    total[...] = jnp.zeros_like(total)

    def step(s, carry):
        for i in range(per):
            block = s * per + i
            weight = w_ref[s, :, i * lanes : (i + 1) * lanes].astype(f32)
            terms = [
                (h_ref[m, pl.ds(block, 1), :] * weight).astype(bf16) for m in range(parts)
            ]
            contrib = jnp.concatenate(terms, axis=0)
            chosen = select_atoms(h_ref, block, atoms)
            slot = dest_ref[block] ^ lax.axis_index("dom")
            total[slot] += lax.dot_general(
                contrib, chosen, (((1,), (1,)), ((), ())), preferred_element_type=f32
            )
        return carry

    lax.fori_loop(0, shards, step, 0)
    for j, out in enumerate(outs):
        out[...] = total[j].astype(out.dtype)


def invariants_kernel(dest_ref, w_ref, h_ref, *refs):
    domains = len(refs) - 3
    out_ref, token_ref, env = refs[domains:]
    token_ref[...] = jnp.zeros_like(token_ref)
    shards, chan, edges = w_ref.shape
    atoms = env.shape[2]
    per = edges // lanes
    for j in range(domains):
        env[j] = refs[j][...]

    def step(s, carry):
        for i in range(per):
            block = s * per + i
            weight = w_ref[s, :, i * lanes : (i + 1) * lanes].astype(f32)
            chosen = select_atoms(h_ref, block, atoms)
            slot = dest_ref[block] ^ lax.axis_index("dom")
            found = jnp.dot(env[slot], chosen, preferred_element_type=f32)
            products = [
                found[m * chan : (m + 1) * chan, :] * h_ref[m, pl.ds(block, 1), :]
                for m in range(parts)
            ]
            at = pl.multiple_of(block * lanes, lanes)
            out_ref[0, :, pl.ds(at, lanes)] = products[0] * weight
            out_ref[1, :, pl.ds(at, lanes)] = sum(products[2:4], products[1]) * weight
            out_ref[2, :, pl.ds(at, lanes)] = sum(products[5:9], products[4]) * weight
        return carry

    lax.fori_loop(0, shards, step, 0)


def on_device(
    latent,
    w_first,
    w_second,
    w_env,
    edge_vec,
    centers,
    block_dest,
    block_fill,
    species,
    species_gain,
):
    domains = lax.axis_size("dom")
    shards = lax.axis_size("tp")
    nblocks = block_fill.shape[0]
    atoms = species.shape[0]
    chan = species_gain.shape[1]
    depth, edges = latent.shape
    spread = (
        depth == lanes
        and w_first.shape[0] % (domains * lanes) == 0
        and w_env.shape[1] % (domains * 16) == 0
        and shards % cores == 0
        and shards & (shards - 1) == 0
        and domains & (domains - 1) == 0
    )
    harmonic = pl.pallas_call(
        geometry_kernel,
        out_shape=jax.ShapeDtypeStruct((parts + 1, nblocks, lanes), f32),
        in_specs=[in_vmem] * 3,
        out_specs=in_vmem,
        compiler_params=grant(4),
        name="geometry",
    )(edge_vec.reshape(3, nblocks, lanes), block_fill[:, None], centers.reshape(nblocks, lanes))
    target = stay(block_dest[:, 0])
    species_ids = jnp.arange(species_gain.shape[0], dtype=jnp.int32)
    gain_sel = jnp.sum(
        jnp.where(
            species[None, None, :] == species_ids[:, None, None], species_gain[:, :, None], 0.0
        ),
        axis=0,
    )
    mlp = spread_mlp if spread else gathered_mlp
    finish, weights, (harmonic, gain_sel) = mlp(
        latent, w_first, w_second, w_env, (harmonic, gain_sel)
    )

    rows = parts * chan
    sums = pl.pallas_call(
        sums_kernel,
        out_shape=[jax.ShapeDtypeStruct((rows, atoms), f32)]
        + [jax.ShapeDtypeStruct((rows, atoms), bf16)] * (domains - 1),
        in_specs=[in_smem] + [in_vmem] * 2,
        out_specs=[in_vmem] * domains,
        scratch_shapes=[pltpu.VMEM((domains, rows, atoms), f32)],
        compiler_params=grant(8),
        name="sums",
    )(target, weights, harmonic)
    env_raw = sums[0]
    for j in range(1, domains):
        env_raw = env_raw + flip_dom(sums[j], j).astype(f32)
    env_out = env_raw.reshape(parts, chan, atoms) * gain_sel[None, :, :] * env_factor
    env_half = env_out.astype(bf16).reshape(rows, atoms)
    looked = [env_half] + [flip_dom(env_half, j) for j in range(1, domains)]
    invariants, token = pl.pallas_call(
        invariants_kernel,
        out_shape=(
            jax.ShapeDtypeStruct((3, chan, edges), f32),
            jax.ShapeDtypeStruct((8, lanes), f32),
        ),
        in_specs=[in_smem] + [in_vmem] * (2 + domains),
        out_specs=(in_vmem, in_vmem),
        scratch_shapes=[pltpu.VMEM((domains, rows, atoms), bf16)],
        compiler_params=grant(10),
        name="invariants",
    )(target, weights, harmonic, *looked)
    return (finish(token), env_out, invariants)


def solution(mesh):
    in_specs = (
        P("tp", "dom"),
        P(None, "tp"),
        P("tp", None),
        P("tp", None),
        P(None, "dom"),
        P("dom"),
        P("dom", None),
        P("dom"),
        P("dom"),
        P(None, "tp"),
    )
    out_specs = (P("tp", "dom"), P(None, "tp", "dom"), P(None, "tp", "dom"))

    return jax.shard_map(on_device, mesh=mesh, in_specs=in_specs, out_specs=out_specs, check_vma=False)
```

```python
import functools
import math

import jax
import jax.numpy as jnp
from jax import lax
from jax.experimental import pallas as pl
from jax.experimental.pallas import tpu as pltpu
from jax.sharding import PartitionSpec as P


root_three = math.sqrt(3.0)
root_five = math.sqrt(5.0)
root_fifteen = math.sqrt(15.0)
cutoff_radius = 6.0
parts = 9
env_factor = 0.25
lanes = 128
cores = 2
bf16 = jnp.bfloat16
f32 = jnp.float32


mib = 1024 * 1024
in_vmem = pl.BlockSpec(memory_space=pltpu.VMEM)
in_smem = pl.BlockSpec(memory_space=pltpu.SMEM)
in_hbm = pl.BlockSpec(memory_space=pltpu.HBM)
anywhere = pl.BlockSpec(memory_space=pl.ANY)


def harmonics(vectors):
    along_x = vectors[0]
    along_y = vectors[1]
    along_z = vectors[2]
    radius = jnp.sqrt(along_x * along_x + along_y * along_y + along_z * along_z)
    unit_x = along_x / radius
    unit_y = along_y / radius
    unit_z = along_z / radius
    ratio = radius / cutoff_radius
    envelope = (1.0 - ratio * ratio) ** 2
    factors = [
        jnp.ones_like(unit_x),
        root_three * unit_x,
        root_three * unit_y,
        root_three * unit_z,
        root_fifteen * unit_x * unit_y,
        root_fifteen * unit_y * unit_z,
        root_five / 2.0 * (3.0 * unit_z * unit_z - 1.0),
        root_fifteen * unit_x * unit_z,
        root_fifteen / 2.0 * (unit_x * unit_x - unit_y * unit_y),
    ]
    return [factor * envelope for factor in factors]


def contract_rows(left, right):
    return lax.dot_general(
        left, right, (((0,), (0,)), ((), ())), preferred_element_type=f32
    )


def swap_blocks(array, axis):
    return lax.all_to_all(array, axis, split_axis=0, concat_axis=0, tiled=True)


def flip_dom(array, mask):
    count = lax.axis_size("dom")
    return lax.ppermute(array, "dom", [(i, i ^ mask) for i in range(count)])


def hop_order(chips):
    return sorted(range(1, chips), key=lambda k: (k.bit_length(), -k))


def flip_tp(array, mask):
    count = lax.axis_size("tp")
    return lax.ppermute(array, "tp", [(t, t ^ mask) for t in range(count)])


def other_core(array):
    return flip_tp(array, 1)


def stay(array):
    return pltpu.with_memory_space_constraint(array, pltpu.HBM)


def grant(size):
    return pltpu.CompilerParams(vmem_limit_bytes=size * mib)


def prepare_kernel(*refs):
    sources, (full_ref, own_ref), held, sems = refs[:3], refs[3:5], refs[5:8], refs[8]
    copies = [
        pltpu.make_async_copy(source, place, sems.at[i])
        for i, (source, place) in enumerate(zip(sources, held))
    ]
    for copy in copies:
        copy.start()
    first_ref, second_ref, env_ref = held
    quarters = full_ref.shape[0]
    width = first_ref.shape[0] // quarters
    chan = env_ref.shape[1] // quarters
    copies[0].wait()
    for q in range(quarters):
        for i in range(width // lanes):
            start = q * width + i * lanes
            full_ref[q, i * lanes : (i + 1) * lanes, :] = first_ref[start : start + lanes, :].T
    copies[1].wait()
    for q in range(quarters):
        full_ref[q, width : 2 * width, :] = second_ref[:, q * width : (q + 1) * width].T
    copies[2].wait()
    for q in range(quarters):
        full_ref[q, 2 * width :, :] = env_ref[:, q * chan : (q + 1) * chan].T
    own_ref[...] = full_ref[lax.axis_index("dom")]


def assemble_kernel(*refs, quarters, order):
    per_group = 1 + len(order) * quarters
    sources = [refs[g * per_group : (g + 1) * per_group] for g in range(cores)]
    first, second, env = refs[cores * per_group :]
    depth = lanes
    width = first.shape[0] // quarters
    chan = env.shape[0] // quarters
    dom = lax.axis_index("dom")
    for k in range(len(order) + 1):
        for g in range(cores):
            at = (k * cores + g) * depth
            for j in range(quarters):
                if k == 0:
                    block = sources[g][0].at[dom ^ j]
                else:
                    block = sources[g][1 + order.index(k) * quarters + j]
                for i in range(width // lanes):
                    column = j * width + i * lanes
                    first[at : at + depth, column : column + lanes] = block[
                        i * depth : (i + 1) * depth, :
                    ]
                row = width // lanes * depth
                start = pl.multiple_of((dom ^ j) * width, lanes)
                second[pl.ds(start, width), at : at + depth] = block[row : row + width, :]
                row += width
                start = pl.multiple_of((dom ^ j) * chan, chan)
                env[pl.ds(start, chan), at : at + depth] = block[row : row + chan, :]


def mlp_kernel(x_ref, *refs, quarters):
    shards, depth, _ = x_ref.shape
    stored, new_refs, out_ref = refs[:3], refs[3 : 3 + shards], refs[3 + shards]
    *held, sems_in, moved, hidden, fresh, rows_out, sems = refs[4 + shards :]
    first, second, env = held
    loads = [
        pltpu.make_async_copy(source, place, sems_in.at[i])
        for i, (source, place) in enumerate(zip(stored, held))
    ]
    for load in loads:
        load.start()
    width = shards * depth // quarters
    per_quarter = shards // quarters
    dom, place = lax.axis_index("dom"), lax.axis_index("tp")
    chip, core = place // cores, lax.rem(place, cores)
    for j in range(quarters):
        for i in range(per_quarter):
            start = j * width + i * depth
            moved[start : start + depth, :] = x_ref[(dom ^ j) * per_quarter + i]
    loads[0].wait()
    value = jnp.dot(first[...], moved[...], preferred_element_type=f32)
    hidden[...] = (value / (1.0 + jnp.exp(-value))).astype(bf16)
    loads[1].wait()
    update = jnp.dot(second[...], hidden[...], preferred_element_type=f32)
    for s in range(shards):
        rows = slice(s * depth, (s + 1) * depth)
        fresh[s] = (x_ref[s].astype(f32) + update[rows, :]).astype(bf16)
    copies = [
        pltpu.make_async_copy(fresh.at[place ^ s], out, sems.at[s])
        for s, out in enumerate(new_refs)
    ]
    for copy in copies:
        copy.start()
    for k in range(shards // cores):
        for g in range(cores):
            at = (k * cores + g) * depth
            moved[at : at + depth, :] = fresh[(chip ^ k) * cores + (core if g == 0 else 1 - core)]
    loads[2].wait()
    rows = jnp.dot(env[...], moved[...], preferred_element_type=f32).astype(bf16)
    per = rows.shape[0] // shards
    for s in range(shards):
        rows_out[s] = rows[s * per : (s + 1) * per, :]
    copies.append(pltpu.make_async_copy(rows_out, out_ref, sems.at[shards]))
    copies[-1].start()
    for copy in copies:
        copy.wait()


def split_kernel(x_ref, tie_ref, out_ref, held, sems_in, sems_out):
    shards, _, edges = held.shape
    arriving = [
        pltpu.make_async_copy(x_ref.at[:, pl.ds(s * edges, edges)], held.at[s], sems_in.at[s])
        for s in range(shards)
    ]
    leaving = [
        pltpu.make_async_copy(held.at[s], out_ref.at[s], sems_out.at[s]) for s in range(shards)
    ]
    for copy in arriving:
        copy.start()
    for before, after in zip(arriving, leaving):
        before.wait()
        after.start()
    for copy in leaving:
        copy.wait()


def join_kernel(tie_ref, *refs):
    pieces, out_ref = refs[:-1], refs[-1]
    edges = pieces[0].shape[1]
    for s, piece in enumerate(pieces):
        at = pl.multiple_of((lax.axis_index("tp") ^ s) * edges, lanes)
        out_ref[:, pl.ds(at, edges)] = piece[...]


def join_pieces(back, tie):
    depth, edges = back[0].shape
    return pl.pallas_call(
        join_kernel,
        out_shape=jax.ShapeDtypeStruct((depth, edges * len(back)), bf16),
        in_specs=[anywhere] + [in_vmem] * len(back),
        out_specs=in_vmem,
        compiler_params=grant(8),
        name="join",
    )(tie, *back)


def spread_mlp(latent, w_first, w_second, w_env, ties):
    domains = lax.axis_size("dom")
    shards = lax.axis_size("tp")
    chips = shards // cores
    total = w_first.shape[0]
    depth = w_first.shape[1]
    channels = w_env.shape[1]
    width = total // domains
    chan = channels // domains
    rows = 2 * width + chan
    edges = latent.shape[1] // shards
    full, own = pl.pallas_call(
        prepare_kernel,
        out_shape=(
            jax.ShapeDtypeStruct((domains, rows, depth), bf16),
            jax.ShapeDtypeStruct((rows, depth), bf16),
        ),
        in_specs=[in_hbm] * 3,
        out_specs=(in_vmem, in_vmem),
        scratch_shapes=[pltpu.VMEM(w.shape, bf16) for w in (w_first, w_second, w_env)]
        + [pltpu.SemaphoreType.DMA((3,))],
        compiler_params=grant(8),
        name="prepare",
    )(stay(w_first), stay(w_second), stay(w_env))
    pieces = pl.pallas_call(
        split_kernel,
        out_shape=pltpu.HBM((shards, depth, edges), bf16),
        in_specs=[in_hbm, anywhere],
        out_specs=in_hbm,
        scratch_shapes=[pltpu.VMEM((shards, depth, edges), bf16)]
        + [pltpu.SemaphoreType.DMA((shards,))] * 2,
        compiler_params=grant(8),
        name="split",
    )(stay(latent), own)
    order = hop_order(chips)
    shifted = {}
    for k in order:
        shifted[k] = flip_tp(own, k * cores)
    edge_rows = swap_blocks(pieces, "tp")
    edge_rows, *ties = lax.optimization_barrier((edge_rows, *ties))
    mine = [full]
    for k in order:
        mine += [shifted[k]] + [flip_dom(shifted[k], j) for j in range(1, domains)]
    others = [other_core(array) for array in mine]
    matrices = pl.pallas_call(
        functools.partial(assemble_kernel, quarters=domains, order=order),
        out_shape=[
            pltpu.HBM((total, total), bf16),
            pltpu.HBM((total, total), bf16),
            pltpu.HBM((channels, total), bf16),
        ],
        in_specs=[in_vmem] * (2 * len(mine)),
        out_specs=[in_vmem] * 3,
        compiler_params=grant(20),
        name="assemble",
    )(*[array if array.ndim == 3 else stay(array) for array in mine + others])
    *new_rows, weight_rows = pl.pallas_call(
        functools.partial(mlp_kernel, quarters=domains),
        out_shape=[pltpu.HBM((depth, edges), bf16)] * shards
        + [pltpu.HBM((shards, channels // shards, edges), bf16)],
        in_specs=[in_vmem] + [in_hbm] * 3,
        out_specs=[in_hbm] * (shards + 1),
        scratch_shapes=[pltpu.VMEM(array.shape, bf16) for array in matrices]
        + [
            pltpu.SemaphoreType.DMA((3,)),
            pltpu.VMEM((total, edges), bf16),
            pltpu.VMEM((total, edges), bf16),
            pltpu.VMEM((shards, depth, edges), bf16),
            pltpu.VMEM((shards, channels // shards, edges), bf16),
            pltpu.SemaphoreType.DMA((shards + 1,)),
        ],
        compiler_params=grant(24),
        name="mlp",
    )(edge_rows, *[stay(array) for array in matrices])
    weights = swap_blocks(weight_rows, "tp")
    back = {0: new_rows[0]}
    for s in range(1, shards):
        back[s] = flip_tp(new_rows[s], s)
    back = [back[s] for s in range(shards)]
    return (lambda tie: join_pieces(back, tie)), weights, ties


def gathered_mlp(latent, w_first, w_second, w_env, ties):
    edge_rows = lax.all_to_all(latent, "tp", split_axis=1, concat_axis=0, tiled=True)
    full_first = lax.all_gather(w_first, "tp", axis=1, tiled=True)
    full_second = lax.all_gather(w_second, "tp", axis=0, tiled=True)
    full_env = lax.all_gather(w_env, "tp", axis=0, tiled=True)
    hidden = jax.nn.silu(contract_rows(full_first, edge_rows)).astype(bf16)
    update = contract_rows(full_second, hidden)
    new_rows = (edge_rows.astype(f32) + update).astype(bf16)
    weight_rows = contract_rows(full_env, new_rows).astype(bf16)
    shards = lax.axis_size("tp")
    weights = swap_blocks(weight_rows.reshape(shards, -1, weight_rows.shape[1]), "tp")
    new_rows, weights = lax.optimization_barrier((new_rows, weights))
    latent_new = lax.all_to_all(new_rows, "tp", split_axis=0, concat_axis=1, tiled=True)
    return (lambda tie: latent_new), weights, ties


def geometry_kernel(vec_ref, fill_ref, centers_ref, out_ref):
    vectors = [vec_ref[i] for i in range(3)]
    ids = lax.broadcasted_iota(jnp.int32, vectors[0].shape, 1)
    alive = (ids < fill_ref[...]).astype(f32)
    for m, part in enumerate(harmonics(vectors)):
        out_ref[m] = part * alive
    out_ref[parts] = centers_ref[...].astype(f32)


def select_atoms(h_ref, block, atoms):
    ids = lax.broadcasted_iota(jnp.int32, (atoms, lanes), 0).astype(f32)
    return (ids == h_ref[parts, pl.ds(block, 1), :]).astype(f32).astype(bf16)


def sums_kernel(dest_ref, w_ref, h_ref, *refs):
    outs, total = refs[:-1], refs[-1]
    shards, _, edges = w_ref.shape
    atoms = total.shape[2]
    per = edges // lanes
    total[...] = jnp.zeros_like(total)

    def step(s, carry):
        for i in range(per):
            block = s * per + i
            weight = w_ref[s, :, i * lanes : (i + 1) * lanes].astype(f32)
            terms = [
                (h_ref[m, pl.ds(block, 1), :] * weight).astype(bf16) for m in range(parts)
            ]
            contrib = jnp.concatenate(terms, axis=0)
            chosen = select_atoms(h_ref, block, atoms)
            slot = dest_ref[block] ^ lax.axis_index("dom")
            total[slot] += lax.dot_general(
                contrib, chosen, (((1,), (1,)), ((), ())), preferred_element_type=f32
            )
        return carry

    lax.fori_loop(0, shards, step, 0)
    for j, out in enumerate(outs):
        out[...] = total[j].astype(out.dtype)


def invariants_kernel(dest_ref, w_ref, h_ref, *refs):
    domains = len(refs) - 5
    result_ref, token_ref, env, out_ref, sems = refs[domains:]
    token_ref[...] = jnp.zeros_like(token_ref)
    shards, chan, edges = w_ref.shape
    atoms = env.shape[2]
    per = edges // lanes
    for j in range(domains):
        env[j] = refs[j][...]

    def step(s, carry):
        for i in range(per):
            block = s * per + i
            weight = w_ref[s, :, i * lanes : (i + 1) * lanes].astype(f32)
            chosen = select_atoms(h_ref, block, atoms)
            slot = dest_ref[block] ^ lax.axis_index("dom")
            found = jnp.dot(env[slot], chosen, preferred_element_type=f32)
            products = [
                found[m * chan : (m + 1) * chan, :] * h_ref[m, pl.ds(block, 1), :]
                for m in range(parts)
            ]
            at = pl.multiple_of(block * lanes, lanes)
            out_ref[0, :, pl.ds(at, lanes)] = products[0] * weight
            out_ref[1, :, pl.ds(at, lanes)] = sum(products[2:4], products[1]) * weight
            out_ref[2, :, pl.ds(at, lanes)] = sum(products[5:9], products[4]) * weight
        leave(s).start()
        return carry

    def leave(s):
        chunk = (slice(None), slice(None), pl.ds(pl.multiple_of(s * edges, lanes), edges))
        return pltpu.make_async_copy(out_ref.at[chunk], result_ref.at[chunk], sems.at[s])

    lax.fori_loop(0, shards, step, 0)
    for s in range(shards):
        leave(s).wait()


def on_device(
    latent,
    w_first,
    w_second,
    w_env,
    edge_vec,
    centers,
    block_dest,
    block_fill,
    species,
    species_gain,
):
    domains = lax.axis_size("dom")
    shards = lax.axis_size("tp")
    nblocks = block_fill.shape[0]
    atoms = species.shape[0]
    chan = species_gain.shape[1]
    depth, edges = latent.shape
    spread = (
        depth == lanes
        and w_first.shape[0] % (domains * lanes) == 0
        and w_env.shape[1] % (domains * 16) == 0
        and shards % cores == 0
        and shards & (shards - 1) == 0
        and domains & (domains - 1) == 0
    )
    harmonic = pl.pallas_call(
        geometry_kernel,
        out_shape=jax.ShapeDtypeStruct((parts + 1, nblocks, lanes), f32),
        in_specs=[in_vmem] * 3,
        out_specs=in_vmem,
        compiler_params=grant(4),
        name="geometry",
    )(edge_vec.reshape(3, nblocks, lanes), block_fill[:, None], centers.reshape(nblocks, lanes))
    target = stay(block_dest[:, 0])
    species_ids = jnp.arange(species_gain.shape[0], dtype=jnp.int32)
    gain_sel = jnp.sum(
        jnp.where(
            species[None, None, :] == species_ids[:, None, None], species_gain[:, :, None], 0.0
        ),
        axis=0,
    )
    mlp = spread_mlp if spread else gathered_mlp
    finish, weights, (harmonic, gain_sel) = mlp(
        latent, w_first, w_second, w_env, (harmonic, gain_sel)
    )

    rows = parts * chan
    sums = pl.pallas_call(
        sums_kernel,
        out_shape=[jax.ShapeDtypeStruct((rows, atoms), f32)]
        + [jax.ShapeDtypeStruct((rows, atoms), bf16)] * (domains - 1),
        in_specs=[in_smem] + [in_vmem] * 2,
        out_specs=[in_vmem] * domains,
        scratch_shapes=[pltpu.VMEM((domains, rows, atoms), f32)],
        compiler_params=grant(8),
        name="sums",
    )(target, weights, harmonic)
    env_raw = sums[0]
    for j in range(1, domains):
        env_raw = env_raw + flip_dom(sums[j], j).astype(f32)
    env_out = env_raw.reshape(parts, chan, atoms) * gain_sel[None, :, :] * env_factor
    env_half = env_out.astype(bf16).reshape(rows, atoms)
    looked = [env_half] + [flip_dom(env_half, j) for j in range(1, domains)]
    invariants, token = pl.pallas_call(
        invariants_kernel,
        out_shape=(
            pltpu.HBM((3, chan, edges), f32),
            jax.ShapeDtypeStruct((8, lanes), f32),
        ),
        in_specs=[in_smem] + [in_vmem] * (2 + domains),
        out_specs=(in_hbm, in_vmem),
        scratch_shapes=[
            pltpu.VMEM((domains, rows, atoms), bf16),
            pltpu.VMEM((3, chan, edges), f32),
            pltpu.SemaphoreType.DMA((shards,)),
        ],
        compiler_params=grant(10),
        name="invariants",
    )(target, weights, harmonic, *looked)
    return (finish(token), env_out, invariants)


def solution(mesh):
    in_specs = (
        P("tp", "dom"),
        P(None, "tp"),
        P("tp", None),
        P("tp", None),
        P(None, "dom"),
        P("dom"),
        P("dom", None),
        P("dom"),
        P("dom"),
        P(None, "tp"),
    )
    out_specs = (P("tp", "dom"), P(None, "tp", "dom"), P(None, "tp", "dom"))

    return jax.shard_map(on_device, mesh=mesh, in_specs=in_specs, out_specs=out_specs, check_vma=False)
```

```python
import functools
import math

import jax
import jax.numpy as jnp
from jax import lax
from jax.experimental import pallas as pl
from jax.experimental.pallas import tpu as pltpu
from jax.sharding import PartitionSpec as P


root_three = math.sqrt(3.0)
root_five = math.sqrt(5.0)
root_fifteen = math.sqrt(15.0)
cutoff_radius = 6.0
parts = 9
env_factor = 0.25
lanes = 128
cores = 2
bf16 = jnp.bfloat16
f32 = jnp.float32


mib = 1024 * 1024
in_vmem = pl.BlockSpec(memory_space=pltpu.VMEM)
in_smem = pl.BlockSpec(memory_space=pltpu.SMEM)
in_hbm = pl.BlockSpec(memory_space=pltpu.HBM)
anywhere = pl.BlockSpec(memory_space=pl.ANY)


def harmonics(vectors):
    along_x = vectors[0]
    along_y = vectors[1]
    along_z = vectors[2]
    radius = jnp.sqrt(along_x * along_x + along_y * along_y + along_z * along_z)
    unit_x = along_x / radius
    unit_y = along_y / radius
    unit_z = along_z / radius
    ratio = radius / cutoff_radius
    envelope = (1.0 - ratio * ratio) ** 2
    factors = [
        jnp.ones_like(unit_x),
        root_three * unit_x,
        root_three * unit_y,
        root_three * unit_z,
        root_fifteen * unit_x * unit_y,
        root_fifteen * unit_y * unit_z,
        root_five / 2.0 * (3.0 * unit_z * unit_z - 1.0),
        root_fifteen * unit_x * unit_z,
        root_fifteen / 2.0 * (unit_x * unit_x - unit_y * unit_y),
    ]
    return [factor * envelope for factor in factors]


def contract_rows(left, right):
    return lax.dot_general(
        left, right, (((0,), (0,)), ((), ())), preferred_element_type=f32
    )


def swap_blocks(array, axis):
    return lax.all_to_all(array, axis, split_axis=0, concat_axis=0, tiled=True)


def flip_dom(array, mask):
    count = lax.axis_size("dom")
    return lax.ppermute(array, "dom", [(i, i ^ mask) for i in range(count)])


def hop_order(chips):
    return sorted(range(1, chips), key=lambda k: (k.bit_length(), -k))


def flip_tp(array, mask):
    count = lax.axis_size("tp")
    return lax.ppermute(array, "tp", [(t, t ^ mask) for t in range(count)])


def other_core(array):
    return flip_tp(array, 1)


def stay(array):
    return pltpu.with_memory_space_constraint(array, pltpu.HBM)


def grant(size):
    return pltpu.CompilerParams(vmem_limit_bytes=size * mib)


def prepare_kernel(*refs):
    sources, (full_ref, own_ref), held, sems = refs[:3], refs[3:5], refs[5:8], refs[8]
    copies = [
        pltpu.make_async_copy(source, place, sems.at[i])
        for i, (source, place) in enumerate(zip(sources, held))
    ]
    for copy in copies:
        copy.start()
    first_ref, second_ref, env_ref = held
    quarters = full_ref.shape[0]
    width = first_ref.shape[0] // quarters
    chan = env_ref.shape[1] // quarters
    copies[0].wait()
    for q in range(quarters):
        for i in range(width // lanes):
            start = q * width + i * lanes
            full_ref[q, i * lanes : (i + 1) * lanes, :] = first_ref[start : start + lanes, :].T
    copies[1].wait()
    for q in range(quarters):
        full_ref[q, width : 2 * width, :] = second_ref[:, q * width : (q + 1) * width].T
    copies[2].wait()
    for q in range(quarters):
        full_ref[q, 2 * width :, :] = env_ref[:, q * chan : (q + 1) * chan].T
    own_ref[...] = full_ref[lax.axis_index("dom")]


def mlp_kernel(x_ref, *refs, quarters, chips, chan, order):
    per_group = 1 + len(order) * quarters
    sources = [refs[g * per_group : (g + 1) * per_group] for g in range(cores)]
    shards, depth, _ = x_ref.shape
    outs = refs[cores * per_group :]
    new_refs, outs = outs[:shards], outs[shards:]
    out_ref, first, second, env, moved, hidden, fresh, rows_out, sems = outs
    total = shards * depth
    width = total // quarters
    per_quarter = shards // quarters
    dom, place = lax.axis_index("dom"), lax.axis_index("tp")
    chip, core = place // cores, lax.rem(place, cores)
    for j in range(quarters):
        for i in range(per_quarter):
            start = j * width + i * depth
            moved[start : start + depth, :] = x_ref[(dom ^ j) * per_quarter + i]
    for k in range(chips):
        for g in range(cores):
            at = (k * cores + g) * depth
            for j in range(quarters):
                if k == 0:
                    block = sources[g][0].at[dom ^ j]
                else:
                    block = sources[g][1 + order.index(k) * quarters + j]
                for i in range(width // lanes):
                    column = j * width + i * lanes
                    first[at : at + depth, column : column + lanes] = block[
                        i * depth : (i + 1) * depth, :
                    ]
                row = width // lanes * depth
                start = pl.multiple_of((dom ^ j) * width, lanes)
                second[pl.ds(start, width), at : at + depth] = block[row : row + width, :]
                row += width
                start = pl.multiple_of((dom ^ j) * chan, chan)
                env[pl.ds(start, chan), at : at + depth] = block[row : row + chan, :]
    value = jnp.dot(first[...], moved[...], preferred_element_type=f32)
    hidden[...] = (value / (1.0 + jnp.exp(-value))).astype(bf16)
    update = jnp.dot(second[...], hidden[...], preferred_element_type=f32)
    for s in range(shards):
        rows = slice(s * depth, (s + 1) * depth)
        fresh[s] = (x_ref[s].astype(f32) + update[rows, :]).astype(bf16)
    copies = [
        pltpu.make_async_copy(fresh.at[place ^ s], out, sems.at[s])
        for s, out in enumerate(new_refs)
    ]
    for copy in copies:
        copy.start()
    for k in range(chips):
        for g in range(cores):
            at = (k * cores + g) * depth
            source = (chip ^ k) * cores + (core if g == 0 else 1 - core)
            moved[at : at + depth, :] = fresh[source]
    rows = jnp.dot(env[...], moved[...], preferred_element_type=f32).astype(bf16)
    per = rows.shape[0] // shards
    for s in range(shards):
        rows_out[s] = rows[s * per : (s + 1) * per, :]
    copies.append(pltpu.make_async_copy(rows_out, out_ref, sems.at[shards]))
    copies[-1].start()
    for copy in copies:
        copy.wait()


def split_kernel(x_ref, tie_ref, out_ref, held, sems_in, sems_out):
    shards, _, edges = held.shape
    arriving = [
        pltpu.make_async_copy(x_ref.at[:, pl.ds(s * edges, edges)], held.at[s], sems_in.at[s])
        for s in range(shards)
    ]
    leaving = [
        pltpu.make_async_copy(held.at[s], out_ref.at[s], sems_out.at[s]) for s in range(shards)
    ]
    for copy in arriving:
        copy.start()
    for before, after in zip(arriving, leaving):
        before.wait()
        after.start()
    for copy in leaving:
        copy.wait()


def join_kernel(tie_ref, *refs):
    pieces, out_ref = refs[:-1], refs[-1]
    edges = pieces[0].shape[1]
    for s, piece in enumerate(pieces):
        at = pl.multiple_of((lax.axis_index("tp") ^ s) * edges, lanes)
        out_ref[:, pl.ds(at, edges)] = piece[...]


def join_pieces(back, tie):
    depth, edges = back[0].shape
    return pl.pallas_call(
        join_kernel,
        out_shape=jax.ShapeDtypeStruct((depth, edges * len(back)), bf16),
        in_specs=[anywhere] + [in_vmem] * len(back),
        out_specs=in_vmem,
        compiler_params=grant(8),
        name="join",
    )(tie, *back)


def spread_mlp(latent, w_first, w_second, w_env, ties):
    domains = lax.axis_size("dom")
    shards = lax.axis_size("tp")
    chips = shards // cores
    total = w_first.shape[0]
    depth = w_first.shape[1]
    channels = w_env.shape[1]
    width = total // domains
    chan = channels // domains
    rows = 2 * width + chan
    edges = latent.shape[1] // shards
    full, own = pl.pallas_call(
        prepare_kernel,
        out_shape=(
            jax.ShapeDtypeStruct((domains, rows, depth), bf16),
            jax.ShapeDtypeStruct((rows, depth), bf16),
        ),
        in_specs=[in_hbm] * 3,
        out_specs=(in_vmem, in_vmem),
        scratch_shapes=[pltpu.VMEM(w.shape, bf16) for w in (w_first, w_second, w_env)]
        + [pltpu.SemaphoreType.DMA((3,))],
        compiler_params=grant(8),
        name="prepare",
    )(stay(w_first), stay(w_second), stay(w_env))
    pieces = pl.pallas_call(
        split_kernel,
        out_shape=pltpu.HBM((shards, depth, edges), bf16),
        in_specs=[in_hbm, anywhere],
        out_specs=in_hbm,
        scratch_shapes=[pltpu.VMEM((shards, depth, edges), bf16)]
        + [pltpu.SemaphoreType.DMA((shards,))] * 2,
        compiler_params=grant(8),
        name="split",
    )(stay(latent), own)
    order = hop_order(chips)
    shifted = {}
    for k in order:
        shifted[k] = flip_tp(own, k * cores)
    edge_rows = swap_blocks(pieces, "tp")
    edge_rows, *ties = lax.optimization_barrier((edge_rows, *ties))
    mine = [full]
    for k in order:
        mine += [shifted[k]] + [flip_dom(shifted[k], j) for j in range(1, domains)]
    others = [other_core(array) for array in mine]
    *new_rows, weight_rows = pl.pallas_call(
        functools.partial(mlp_kernel, quarters=domains, chips=chips, chan=chan, order=order),
        out_shape=[pltpu.HBM((depth, edges), bf16)] * shards
        + [pltpu.HBM((shards, channels // shards, edges), bf16)],
        in_specs=[in_vmem] * (1 + 2 * len(mine)),
        out_specs=[in_hbm] * (shards + 1),
        scratch_shapes=[
            pltpu.VMEM((total, total), bf16),
            pltpu.VMEM((total, total), bf16),
            pltpu.VMEM((channels, total), bf16),
            pltpu.VMEM((total, edges), bf16),
            pltpu.VMEM((total, edges), bf16),
            pltpu.VMEM((shards, depth, edges), bf16),
            pltpu.VMEM((shards, channels // shards, edges), bf16),
            pltpu.SemaphoreType.DMA((shards + 1,)),
        ],
        compiler_params=grant(28),
        name="mlp",
    )(edge_rows, *mine, *others)
    weights = swap_blocks(weight_rows, "tp")
    back = {0: new_rows[0]}
    for s in range(1, shards):
        back[s] = flip_tp(new_rows[s], s)
    back = [back[s] for s in range(shards)]
    return (lambda tie: join_pieces(back, tie)), weights, ties


def gathered_mlp(latent, w_first, w_second, w_env, ties):
    edge_rows = lax.all_to_all(latent, "tp", split_axis=1, concat_axis=0, tiled=True)
    full_first = lax.all_gather(w_first, "tp", axis=1, tiled=True)
    full_second = lax.all_gather(w_second, "tp", axis=0, tiled=True)
    full_env = lax.all_gather(w_env, "tp", axis=0, tiled=True)
    hidden = jax.nn.silu(contract_rows(full_first, edge_rows)).astype(bf16)
    update = contract_rows(full_second, hidden)
    new_rows = (edge_rows.astype(f32) + update).astype(bf16)
    weight_rows = contract_rows(full_env, new_rows).astype(bf16)
    shards = lax.axis_size("tp")
    weights = swap_blocks(weight_rows.reshape(shards, -1, weight_rows.shape[1]), "tp")
    new_rows, weights = lax.optimization_barrier((new_rows, weights))
    latent_new = lax.all_to_all(new_rows, "tp", split_axis=0, concat_axis=1, tiled=True)
    return (lambda tie: latent_new), weights, ties


def geometry_kernel(fill_ref, table_ref, vec_ref, centers_ref, species_ref, out_ref, gain_ref, rows):
    species_count, chan = table_ref.shape
    for b in range(centers_ref.shape[0]):
        rows[:, b, :] = vec_ref[:, b * lanes : (b + 1) * lanes]
        ids = lax.broadcasted_iota(jnp.int32, (1, lanes), 1)
        out_ref[parts, b : b + 1, :] = (ids < fill_ref[b]).astype(f32)
    alive = out_ref[parts]
    for m, part in enumerate(harmonics([rows[i] for i in range(3)])):
        out_ref[m] = part * alive
    out_ref[parts] = centers_ref[...].astype(f32)
    species = species_ref[...]
    for c in range(chan):
        gain = jnp.zeros(species.shape, f32)
        for kind in range(species_count):
            gain = jnp.where(species == kind, table_ref[kind, c], gain)
        gain_ref[c : c + 1, :] = gain


def select_atoms(h_ref, block, atoms):
    ids = lax.broadcasted_iota(jnp.int32, (atoms, lanes), 0).astype(f32)
    return (ids == h_ref[parts, pl.ds(block, 1), :]).astype(f32).astype(bf16)


def sums_kernel(dest_ref, w_ref, h_ref, *refs):
    outs, total = refs[:-1], refs[-1]
    shards, _, edges = w_ref.shape
    atoms = total.shape[2]
    per = edges // lanes
    total[...] = jnp.zeros_like(total)

    def step(s, carry):
        for i in range(per):
            block = s * per + i
            weight = w_ref[s, :, i * lanes : (i + 1) * lanes].astype(f32)
            terms = [
                (h_ref[m, pl.ds(block, 1), :] * weight).astype(bf16) for m in range(parts)
            ]
            contrib = jnp.concatenate(terms, axis=0)
            chosen = select_atoms(h_ref, block, atoms)
            slot = dest_ref[block] ^ lax.axis_index("dom")
            total[slot] += lax.dot_general(
                contrib, chosen, (((1,), (1,)), ((), ())), preferred_element_type=f32
            )
        return carry

    lax.fori_loop(0, shards, step, 0)
    for j, out in enumerate(outs):
        out[...] = total[j].astype(out.dtype)


def invariants_kernel(dest_ref, w_ref, h_ref, *refs):
    domains = len(refs) - 5
    result_ref, token_ref, env, out_ref, sems = refs[domains:]
    token_ref[...] = jnp.zeros_like(token_ref)
    shards, chan, edges = w_ref.shape
    atoms = env.shape[2]
    per = edges // lanes
    for j in range(domains):
        env[j] = refs[j][...]

    def step(s, carry):
        for i in range(per):
            block = s * per + i
            weight = w_ref[s, :, i * lanes : (i + 1) * lanes].astype(f32)
            chosen = select_atoms(h_ref, block, atoms)
            slot = dest_ref[block] ^ lax.axis_index("dom")
            found = jnp.dot(env[slot], chosen, preferred_element_type=f32)
            products = [
                found[m * chan : (m + 1) * chan, :] * h_ref[m, pl.ds(block, 1), :]
                for m in range(parts)
            ]
            at = pl.multiple_of(block * lanes, lanes)
            out_ref[0, :, pl.ds(at, lanes)] = products[0] * weight
            out_ref[1, :, pl.ds(at, lanes)] = sum(products[2:4], products[1]) * weight
            out_ref[2, :, pl.ds(at, lanes)] = sum(products[5:9], products[4]) * weight
        leave(s).start()
        return carry

    def leave(s):
        chunk = (slice(None), slice(None), pl.ds(pl.multiple_of(s * edges, lanes), edges))
        return pltpu.make_async_copy(out_ref.at[chunk], result_ref.at[chunk], sems.at[s])

    lax.fori_loop(0, shards, step, 0)
    for s in range(shards):
        leave(s).wait()


def on_device(
    latent,
    w_first,
    w_second,
    w_env,
    edge_vec,
    centers,
    block_dest,
    block_fill,
    species,
    species_gain,
):
    domains = lax.axis_size("dom")
    shards = lax.axis_size("tp")
    nblocks = block_fill.shape[0]
    atoms = species.shape[0]
    chan = species_gain.shape[1]
    depth, edges = latent.shape
    spread = (
        depth == lanes
        and w_first.shape[0] % (domains * lanes) == 0
        and w_env.shape[1] % (domains * 16) == 0
        and shards % cores == 0
        and shards & (shards - 1) == 0
        and domains & (domains - 1) == 0
    )
    harmonic, gain_sel = pl.pallas_call(
        geometry_kernel,
        out_shape=(
            jax.ShapeDtypeStruct((parts + 1, nblocks, lanes), f32),
            jax.ShapeDtypeStruct((chan, atoms), f32),
        ),
        in_specs=[in_smem] * 2 + [in_vmem] * 3,
        out_specs=(in_vmem, in_vmem),
        scratch_shapes=[pltpu.VMEM((3, nblocks, lanes), f32)],
        compiler_params=grant(4),
        name="geometry",
    )(
        stay(block_fill),
        stay(species_gain),
        edge_vec,
        centers.reshape(nblocks, lanes),
        species[None, :],
    )
    target = stay(block_dest[:, 0])
    mlp = spread_mlp if spread else gathered_mlp
    finish, weights, (harmonic, gain_sel) = mlp(
        latent, w_first, w_second, w_env, (harmonic, gain_sel)
    )

    rows = parts * chan
    sums = pl.pallas_call(
        sums_kernel,
        out_shape=[jax.ShapeDtypeStruct((rows, atoms), f32)]
        + [jax.ShapeDtypeStruct((rows, atoms), bf16)] * (domains - 1),
        in_specs=[in_smem] + [in_vmem] * 2,
        out_specs=[in_vmem] * domains,
        scratch_shapes=[pltpu.VMEM((domains, rows, atoms), f32)],
        compiler_params=grant(8),
        name="sums",
    )(target, weights, harmonic)
    env_raw = sums[0]
    for j in range(1, domains):
        env_raw = env_raw + flip_dom(sums[j], j).astype(f32)
    env_out = env_raw.reshape(parts, chan, atoms) * gain_sel[None, :, :] * env_factor
    env_half = env_out.astype(bf16).reshape(rows, atoms)
    looked = [env_half] + [flip_dom(env_half, j) for j in range(1, domains)]
    invariants, token = pl.pallas_call(
        invariants_kernel,
        out_shape=(
            pltpu.HBM((3, chan, edges), f32),
            jax.ShapeDtypeStruct((8, lanes), f32),
        ),
        in_specs=[in_smem] + [in_vmem] * (2 + domains),
        out_specs=(in_hbm, in_vmem),
        scratch_shapes=[
            pltpu.VMEM((domains, rows, atoms), bf16),
            pltpu.VMEM((3, chan, edges), f32),
            pltpu.SemaphoreType.DMA((shards,)),
        ],
        compiler_params=grant(10),
        name="invariants",
    )(target, weights, harmonic, *looked)
    return (finish(token), env_out, invariants)


def solution(mesh):
    in_specs = (
        P("tp", "dom"),
        P(None, "tp"),
        P("tp", None),
        P("tp", None),
        P(None, "dom"),
        P("dom"),
        P("dom", None),
        P("dom"),
        P("dom"),
        P(None, "tp"),
    )
    out_specs = (P("tp", "dom"), P(None, "tp", "dom"), P(None, "tp", "dom"))

    return jax.shard_map(on_device, mesh=mesh, in_specs=in_specs, out_specs=out_specs, check_vma=False)
```

```python
import functools
import math

import jax
import jax.numpy as jnp
from jax import lax
from jax.experimental import pallas as pl
from jax.experimental.pallas import tpu as pltpu
from jax.sharding import PartitionSpec as P


root_three = math.sqrt(3.0)
root_five = math.sqrt(5.0)
root_fifteen = math.sqrt(15.0)
cutoff_radius = 6.0
parts = 9
env_factor = 0.25
lanes = 128
cores = 2
bf16 = jnp.bfloat16
f32 = jnp.float32


mib = 1024 * 1024
in_vmem = pl.BlockSpec(memory_space=pltpu.VMEM)
in_smem = pl.BlockSpec(memory_space=pltpu.SMEM)
in_hbm = pl.BlockSpec(memory_space=pltpu.HBM)
anywhere = pl.BlockSpec(memory_space=pl.ANY)


def harmonics(vectors):
    along_x = vectors[0]
    along_y = vectors[1]
    along_z = vectors[2]
    radius = jnp.sqrt(along_x * along_x + along_y * along_y + along_z * along_z)
    unit_x = along_x / radius
    unit_y = along_y / radius
    unit_z = along_z / radius
    ratio = radius / cutoff_radius
    envelope = (1.0 - ratio * ratio) ** 2
    factors = [
        jnp.ones_like(unit_x),
        root_three * unit_x,
        root_three * unit_y,
        root_three * unit_z,
        root_fifteen * unit_x * unit_y,
        root_fifteen * unit_y * unit_z,
        root_five / 2.0 * (3.0 * unit_z * unit_z - 1.0),
        root_fifteen * unit_x * unit_z,
        root_fifteen / 2.0 * (unit_x * unit_x - unit_y * unit_y),
    ]
    return [factor * envelope for factor in factors]


def contract_rows(left, right):
    return lax.dot_general(
        left, right, (((0,), (0,)), ((), ())), preferred_element_type=f32
    )


def swap_blocks(array, axis):
    return lax.all_to_all(array, axis, split_axis=0, concat_axis=0, tiled=True)


def flip_dom(array, mask):
    count = lax.axis_size("dom")
    return lax.ppermute(array, "dom", [(i, i ^ mask) for i in range(count)])


def send_chips(array, moves):
    pairs = [(a * cores + c, b * cores + c) for a, b in moves for c in range(cores)]
    return lax.ppermute(array, "tp", pairs)


def flip_tp(array, mask):
    count = lax.axis_size("tp")
    return lax.ppermute(array, "tp", [(t, t ^ mask) for t in range(count)])


def other_core(array):
    return flip_tp(array, 1)


def stay(array):
    return pltpu.with_memory_space_constraint(array, pltpu.HBM)


def grant(size):
    return pltpu.CompilerParams(vmem_limit_bytes=size * mib)


def prepare_kernel(*refs):
    sources, (full_ref, own_ref), held, sems = refs[:3], refs[3:5], refs[5:8], refs[8]
    copies = [
        pltpu.make_async_copy(source, place, sems.at[i])
        for i, (source, place) in enumerate(zip(sources, held))
    ]
    for copy in copies:
        copy.start()
    first_ref, second_ref, env_ref = held
    quarters = full_ref.shape[0]
    width = first_ref.shape[0] // quarters
    chan = env_ref.shape[1] // quarters
    copies[0].wait()
    for q in range(quarters):
        for i in range(width // lanes):
            start = q * width + i * lanes
            full_ref[q, i * lanes : (i + 1) * lanes, :] = first_ref[start : start + lanes, :].T
    copies[1].wait()
    for q in range(quarters):
        full_ref[q, width : 2 * width, :] = second_ref[:, q * width : (q + 1) * width].T
    copies[2].wait()
    for q in range(quarters):
        full_ref[q, 2 * width :, :] = env_ref[:, q * chan : (q + 1) * chan].T
    own_ref[...] = full_ref[lax.axis_index("dom")]


def mlp_kernel(x_ref, *refs, quarters, chips, chan):
    per_group = 1 + (chips - 1) * quarters
    sources = [refs[g * per_group : (g + 1) * per_group] for g in range(cores)]
    shards, depth, _ = x_ref.shape
    outs = refs[cores * per_group :]
    new_refs, outs = outs[:shards], outs[shards:]
    out_ref, first, second, env, moved, hidden, fresh, rows_out, sems = outs
    total = shards * depth
    width = total // quarters
    per_quarter = shards // quarters
    dom, place = lax.axis_index("dom"), lax.axis_index("tp")
    chip, core = place // cores, lax.rem(place, cores)
    for j in range(quarters):
        for i in range(per_quarter):
            start = j * width + i * depth
            moved[start : start + depth, :] = x_ref[(dom ^ j) * per_quarter + i]
    for k in range(chips):
        for g in range(cores):
            at = (k * cores + g) * depth
            for j in range(quarters):
                if k == 0:
                    block = sources[g][0].at[dom ^ j]
                else:
                    block = sources[g][1 + (k - 1) * quarters + j]
                for i in range(width // lanes):
                    column = j * width + i * lanes
                    first[at : at + depth, column : column + lanes] = block[
                        i * depth : (i + 1) * depth, :
                    ]
                row = width // lanes * depth
                start = pl.multiple_of((dom ^ j) * width, lanes)
                second[pl.ds(start, width), at : at + depth] = block[row : row + width, :]
                row += width
                start = pl.multiple_of((dom ^ j) * chan, chan)
                env[pl.ds(start, chan), at : at + depth] = block[row : row + chan, :]
    value = jnp.dot(first[...], moved[...], preferred_element_type=f32)
    hidden[...] = (value / (1.0 + jnp.exp(-value))).astype(bf16)
    update = jnp.dot(second[...], hidden[...], preferred_element_type=f32)
    for s in range(shards):
        rows = slice(s * depth, (s + 1) * depth)
        fresh[s] = (x_ref[s].astype(f32) + update[rows, :]).astype(bf16)
    copies = [
        pltpu.make_async_copy(fresh.at[place ^ s], out, sems.at[s])
        for s, out in enumerate(new_refs)
    ]
    for copy in copies:
        copy.start()
    left = chip < 2
    origins = (chip, chip ^ 1, jnp.where(left, 2, 1), jnp.where(left, 3, 0))
    for k in range(chips):
        for g in range(cores):
            at = (k * cores + g) * depth
            source = origins[k] * cores + (core if g == 0 else 1 - core)
            moved[at : at + depth, :] = fresh[source]
    rows = jnp.dot(env[...], moved[...], preferred_element_type=f32).astype(bf16)
    per = rows.shape[0] // shards
    for s in range(shards):
        rows_out[s] = rows[s * per : (s + 1) * per, :]
    copies.append(pltpu.make_async_copy(rows_out, out_ref, sems.at[shards]))
    copies[-1].start()
    for copy in copies:
        copy.wait()


def split_kernel(x_ref, tie_ref, out_ref, held, sems_in, sems_out):
    shards, _, edges = held.shape
    arriving = [
        pltpu.make_async_copy(x_ref.at[:, pl.ds(s * edges, edges)], held.at[s], sems_in.at[s])
        for s in range(shards)
    ]
    leaving = [
        pltpu.make_async_copy(held.at[s], out_ref.at[s], sems_out.at[s]) for s in range(shards)
    ]
    for copy in arriving:
        copy.start()
    for before, after in zip(arriving, leaving):
        before.wait()
        after.start()
    for copy in leaving:
        copy.wait()


def join_kernel(tie_ref, *refs):
    pieces, out_ref = refs[:-1], refs[-1]
    edges = pieces[0].shape[1]
    for s, piece in enumerate(pieces):
        at = pl.multiple_of((lax.axis_index("tp") ^ s) * edges, lanes)
        out_ref[:, pl.ds(at, edges)] = piece[...]


def join_pieces(back, tie):
    depth, edges = back[0].shape
    return pl.pallas_call(
        join_kernel,
        out_shape=jax.ShapeDtypeStruct((depth, edges * len(back)), bf16),
        in_specs=[anywhere] + [in_vmem] * len(back),
        out_specs=in_vmem,
        compiler_params=grant(8),
        name="join",
    )(tie, *back)


def spread_mlp(latent, w_first, w_second, w_env, ties):
    domains = lax.axis_size("dom")
    shards = lax.axis_size("tp")
    chips = shards // cores
    total = w_first.shape[0]
    depth = w_first.shape[1]
    channels = w_env.shape[1]
    width = total // domains
    chan = channels // domains
    rows = 2 * width + chan
    edges = latent.shape[1] // shards
    full, own = pl.pallas_call(
        prepare_kernel,
        out_shape=(
            jax.ShapeDtypeStruct((domains, rows, depth), bf16),
            jax.ShapeDtypeStruct((rows, depth), bf16),
        ),
        in_specs=[in_hbm] * 3,
        out_specs=(in_vmem, in_vmem),
        scratch_shapes=[pltpu.VMEM(w.shape, bf16) for w in (w_first, w_second, w_env)]
        + [pltpu.SemaphoreType.DMA((3,))],
        compiler_params=grant(8),
        name="prepare",
    )(stay(w_first), stay(w_second), stay(w_env))
    pieces = pl.pallas_call(
        split_kernel,
        out_shape=pltpu.HBM((shards, depth, edges), bf16),
        in_specs=[in_hbm, anywhere],
        out_specs=in_hbm,
        scratch_shapes=[pltpu.VMEM((shards, depth, edges), bf16)]
        + [pltpu.SemaphoreType.DMA((shards,))] * 2,
        compiler_params=grant(8),
        name="split",
    )(stay(latent), own)
    last = chips - 1
    across, outward = [(1, 2), (2, 1)], [(1, 0), (2, last)]
    beside = flip_tp(own, cores)
    near = send_chips(own, across)
    far = send_chips(own, [(0, last), (last, 0)])
    far = far + send_chips(own, [(0, 2), (last, 1)])
    near = near + send_chips(near, outward)
    edge_rows = swap_blocks(pieces, "tp")
    edge_rows, *ties = lax.optimization_barrier((edge_rows, *ties))
    mine = [full]
    for piece in (beside, near, far):
        mine += [piece] + [flip_dom(piece, j) for j in range(1, domains)]
    others = [other_core(array) for array in mine]
    *new_rows, weight_rows = pl.pallas_call(
        functools.partial(mlp_kernel, quarters=domains, chips=chips, chan=chan),
        out_shape=[pltpu.HBM((depth, edges), bf16)] * shards
        + [pltpu.HBM((shards, channels // shards, edges), bf16)],
        in_specs=[in_vmem] * (1 + 2 * len(mine)),
        out_specs=[in_hbm] * (shards + 1),
        scratch_shapes=[
            pltpu.VMEM((total, total), bf16),
            pltpu.VMEM((total, total), bf16),
            pltpu.VMEM((channels, total), bf16),
            pltpu.VMEM((total, edges), bf16),
            pltpu.VMEM((total, edges), bf16),
            pltpu.VMEM((shards, depth, edges), bf16),
            pltpu.VMEM((shards, channels // shards, edges), bf16),
            pltpu.SemaphoreType.DMA((shards + 1,)),
        ],
        compiler_params=grant(28),
        name="mlp",
    )(edge_rows, *mine, *others)
    weights = swap_blocks(weight_rows, "tp")
    back = {0: new_rows[0]}
    for s in range(1, shards):
        back[s] = flip_tp(new_rows[s], s)
    back = [back[s] for s in range(shards)]
    return (lambda tie: join_pieces(back, tie)), weights, ties


def gathered_mlp(latent, w_first, w_second, w_env, ties):
    edge_rows = lax.all_to_all(latent, "tp", split_axis=1, concat_axis=0, tiled=True)
    full_first = lax.all_gather(w_first, "tp", axis=1, tiled=True)
    full_second = lax.all_gather(w_second, "tp", axis=0, tiled=True)
    full_env = lax.all_gather(w_env, "tp", axis=0, tiled=True)
    hidden = jax.nn.silu(contract_rows(full_first, edge_rows)).astype(bf16)
    update = contract_rows(full_second, hidden)
    new_rows = (edge_rows.astype(f32) + update).astype(bf16)
    weight_rows = contract_rows(full_env, new_rows).astype(bf16)
    shards = lax.axis_size("tp")
    weights = swap_blocks(weight_rows.reshape(shards, -1, weight_rows.shape[1]), "tp")
    new_rows, weights = lax.optimization_barrier((new_rows, weights))
    latent_new = lax.all_to_all(new_rows, "tp", split_axis=0, concat_axis=1, tiled=True)
    return (lambda tie: latent_new), weights, ties


def geometry_kernel(fill_ref, table_ref, vec_ref, centers_ref, species_ref, out_ref, gain_ref, rows):
    species_count, chan = table_ref.shape
    for b in range(centers_ref.shape[0]):
        rows[:, b, :] = vec_ref[:, b * lanes : (b + 1) * lanes]
        ids = lax.broadcasted_iota(jnp.int32, (1, lanes), 1)
        out_ref[parts, b : b + 1, :] = (ids < fill_ref[b]).astype(f32)
    alive = out_ref[parts]
    for m, part in enumerate(harmonics([rows[i] for i in range(3)])):
        out_ref[m] = part * alive
    out_ref[parts] = centers_ref[...].astype(f32)
    species = species_ref[...]
    for c in range(chan):
        gain = jnp.zeros(species.shape, f32)
        for kind in range(species_count):
            gain = jnp.where(species == kind, table_ref[kind, c], gain)
        gain_ref[c : c + 1, :] = gain


def select_atoms(h_ref, block, atoms):
    ids = lax.broadcasted_iota(jnp.int32, (atoms, lanes), 0).astype(f32)
    return (ids == h_ref[parts, pl.ds(block, 1), :]).astype(f32).astype(bf16)


def sums_kernel(dest_ref, w_ref, h_ref, *refs):
    outs, total = refs[:-1], refs[-1]
    shards, _, edges = w_ref.shape
    atoms = total.shape[2]
    per = edges // lanes
    total[...] = jnp.zeros_like(total)

    def step(s, carry):
        for i in range(per):
            block = s * per + i
            weight = w_ref[s, :, i * lanes : (i + 1) * lanes].astype(f32)
            terms = [
                (h_ref[m, pl.ds(block, 1), :] * weight).astype(bf16) for m in range(parts)
            ]
            contrib = jnp.concatenate(terms, axis=0)
            chosen = select_atoms(h_ref, block, atoms)
            slot = dest_ref[block] ^ lax.axis_index("dom")
            total[slot] += lax.dot_general(
                contrib, chosen, (((1,), (1,)), ((), ())), preferred_element_type=f32
            )
        return carry

    lax.fori_loop(0, shards, step, 0)
    for j, out in enumerate(outs):
        out[...] = total[j].astype(out.dtype)


def invariants_kernel(dest_ref, w_ref, h_ref, *refs):
    domains = len(refs) - 5
    result_ref, token_ref, env, out_ref, sems = refs[domains:]
    token_ref[...] = jnp.zeros_like(token_ref)
    shards, chan, edges = w_ref.shape
    atoms = env.shape[2]
    per = edges // lanes
    for j in range(domains):
        env[j] = refs[j][...]

    def step(s, carry):
        for i in range(per):
            block = s * per + i
            weight = w_ref[s, :, i * lanes : (i + 1) * lanes].astype(f32)
            chosen = select_atoms(h_ref, block, atoms)
            slot = dest_ref[block] ^ lax.axis_index("dom")
            found = jnp.dot(env[slot], chosen, preferred_element_type=f32)
            products = [
                found[m * chan : (m + 1) * chan, :] * h_ref[m, pl.ds(block, 1), :]
                for m in range(parts)
            ]
            at = pl.multiple_of(block * lanes, lanes)
            out_ref[0, :, pl.ds(at, lanes)] = products[0] * weight
            out_ref[1, :, pl.ds(at, lanes)] = sum(products[2:4], products[1]) * weight
            out_ref[2, :, pl.ds(at, lanes)] = sum(products[5:9], products[4]) * weight
        leave(s).start()
        return carry

    def leave(s):
        chunk = (slice(None), slice(None), pl.ds(pl.multiple_of(s * edges, lanes), edges))
        return pltpu.make_async_copy(out_ref.at[chunk], result_ref.at[chunk], sems.at[s])

    lax.fori_loop(0, shards, step, 0)
    for s in range(shards):
        leave(s).wait()


def on_device(
    latent,
    w_first,
    w_second,
    w_env,
    edge_vec,
    centers,
    block_dest,
    block_fill,
    species,
    species_gain,
):
    domains = lax.axis_size("dom")
    shards = lax.axis_size("tp")
    nblocks = block_fill.shape[0]
    atoms = species.shape[0]
    chan = species_gain.shape[1]
    depth, edges = latent.shape
    spread = (
        depth == lanes
        and w_first.shape[0] % (domains * lanes) == 0
        and w_env.shape[1] % (domains * 16) == 0
        and shards % cores == 0
        and shards == 4 * cores
        and domains & (domains - 1) == 0
    )
    harmonic, gain_sel = pl.pallas_call(
        geometry_kernel,
        out_shape=(
            jax.ShapeDtypeStruct((parts + 1, nblocks, lanes), f32),
            jax.ShapeDtypeStruct((chan, atoms), f32),
        ),
        in_specs=[in_smem] * 2 + [in_vmem] * 3,
        out_specs=(in_vmem, in_vmem),
        scratch_shapes=[pltpu.VMEM((3, nblocks, lanes), f32)],
        compiler_params=grant(4),
        name="geometry",
    )(
        stay(block_fill),
        stay(species_gain),
        edge_vec,
        centers.reshape(nblocks, lanes),
        species[None, :],
    )
    target = stay(block_dest[:, 0])
    mlp = spread_mlp if spread else gathered_mlp
    finish, weights, (harmonic, gain_sel) = mlp(
        latent, w_first, w_second, w_env, (harmonic, gain_sel)
    )

    rows = parts * chan
    sums = pl.pallas_call(
        sums_kernel,
        out_shape=[jax.ShapeDtypeStruct((rows, atoms), f32)]
        + [jax.ShapeDtypeStruct((rows, atoms), bf16)] * (domains - 1),
        in_specs=[in_smem] + [in_vmem] * 2,
        out_specs=[in_vmem] * domains,
        scratch_shapes=[pltpu.VMEM((domains, rows, atoms), f32)],
        compiler_params=grant(8),
        name="sums",
    )(target, weights, harmonic)
    env_raw = sums[0]
    for j in range(1, domains):
        env_raw = env_raw + flip_dom(sums[j], j).astype(f32)
    env_out = env_raw.reshape(parts, chan, atoms) * gain_sel[None, :, :] * env_factor
    env_half = env_out.astype(bf16).reshape(rows, atoms)
    looked = [env_half] + [flip_dom(env_half, j) for j in range(1, domains)]
    invariants, token = pl.pallas_call(
        invariants_kernel,
        out_shape=(
            pltpu.HBM((3, chan, edges), f32),
            jax.ShapeDtypeStruct((8, lanes), f32),
        ),
        in_specs=[in_smem] + [in_vmem] * (2 + domains),
        out_specs=(in_hbm, in_vmem),
        scratch_shapes=[
            pltpu.VMEM((domains, rows, atoms), bf16),
            pltpu.VMEM((3, chan, edges), f32),
            pltpu.SemaphoreType.DMA((shards,)),
        ],
        compiler_params=grant(10),
        name="invariants",
    )(target, weights, harmonic, *looked)
    return (finish(token), env_out, invariants)


def solution(mesh):
    in_specs = (
        P("tp", "dom"),
        P(None, "tp"),
        P("tp", None),
        P("tp", None),
        P(None, "dom"),
        P("dom"),
        P("dom", None),
        P("dom"),
        P("dom"),
        P(None, "tp"),
    )
    out_specs = (P("tp", "dom"), P(None, "tp", "dom"), P(None, "tp", "dom"))

    return jax.shard_map(on_device, mesh=mesh, in_specs=in_specs, out_specs=out_specs, check_vma=False)
```

```python
import functools
import math

import jax
import jax.numpy as jnp
from jax import lax
from jax.experimental import pallas as pl
from jax.experimental.pallas import tpu as pltpu
from jax.sharding import PartitionSpec as P


root_three = math.sqrt(3.0)
root_five = math.sqrt(5.0)
root_fifteen = math.sqrt(15.0)
cutoff_radius = 6.0
parts = 9
env_factor = 0.25
lanes = 128
cores = 2
bf16 = jnp.bfloat16
f32 = jnp.float32


mib = 1024 * 1024
in_vmem = pl.BlockSpec(memory_space=pltpu.VMEM)
in_smem = pl.BlockSpec(memory_space=pltpu.SMEM)
in_hbm = pl.BlockSpec(memory_space=pltpu.HBM)
anywhere = pl.BlockSpec(memory_space=pl.ANY)


def harmonics(vectors):
    along_x = vectors[0]
    along_y = vectors[1]
    along_z = vectors[2]
    radius = jnp.sqrt(along_x * along_x + along_y * along_y + along_z * along_z)
    unit_x = along_x / radius
    unit_y = along_y / radius
    unit_z = along_z / radius
    ratio = radius / cutoff_radius
    envelope = (1.0 - ratio * ratio) ** 2
    factors = [
        jnp.ones_like(unit_x),
        root_three * unit_x,
        root_three * unit_y,
        root_three * unit_z,
        root_fifteen * unit_x * unit_y,
        root_fifteen * unit_y * unit_z,
        root_five / 2.0 * (3.0 * unit_z * unit_z - 1.0),
        root_fifteen * unit_x * unit_z,
        root_fifteen / 2.0 * (unit_x * unit_x - unit_y * unit_y),
    ]
    return [factor * envelope for factor in factors]


def contract_rows(left, right):
    return lax.dot_general(
        left, right, (((0,), (0,)), ((), ())), preferred_element_type=f32
    )


def swap_blocks(array, axis):
    return lax.all_to_all(array, axis, split_axis=0, concat_axis=0, tiled=True)


def flip_dom(array, mask):
    count = lax.axis_size("dom")
    return lax.ppermute(array, "dom", [(i, i ^ mask) for i in range(count)])


def hop_order(chips):
    return sorted(range(1, chips), key=lambda k: (k.bit_length(), -k))


def flip_tp(array, mask):
    count = lax.axis_size("tp")
    return lax.ppermute(array, "tp", [(t, t ^ mask) for t in range(count)])


def other_core(array):
    return flip_tp(array, 1)


def stay(array):
    return pltpu.with_memory_space_constraint(array, pltpu.HBM)


def grant(size):
    return pltpu.CompilerParams(vmem_limit_bytes=size * mib)


def prepare_kernel(*refs):
    sources, (full_ref, own_ref), held, sems = refs[:3], refs[3:5], refs[5:8], refs[8]
    copies = [
        pltpu.make_async_copy(source, place, sems.at[i])
        for i, (source, place) in enumerate(zip(sources, held))
    ]
    for copy in copies:
        copy.start()
    first_ref, second_ref, env_ref = held
    quarters = full_ref.shape[0]
    width = first_ref.shape[0] // quarters
    chan = env_ref.shape[1] // quarters
    copies[0].wait()
    for q in range(quarters):
        for i in range(width // lanes):
            start = q * width + i * lanes
            full_ref[q, i * lanes : (i + 1) * lanes, :] = first_ref[start : start + lanes, :].T
    copies[1].wait()
    for q in range(quarters):
        full_ref[q, width : 2 * width, :] = second_ref[:, q * width : (q + 1) * width].T
    copies[2].wait()
    for q in range(quarters):
        full_ref[q, 2 * width :, :] = env_ref[:, q * chan : (q + 1) * chan].T
    own_ref[...] = full_ref[lax.axis_index("dom")]


def mlp_kernel(x_ref, *refs, quarters, chips, chan, order):
    per_group = 1 + len(order) * quarters
    sources = [refs[g * per_group : (g + 1) * per_group] for g in range(cores)]
    shards, depth, _ = x_ref.shape
    outs = refs[cores * per_group :]
    new_refs, outs = outs[:shards], outs[shards:]
    out_ref, first, second, env, moved, hidden, fresh, rows_out, sems = outs
    total = shards * depth
    width = total // quarters
    per_quarter = shards // quarters
    dom, place = lax.axis_index("dom"), lax.axis_index("tp")
    chip, core = place // cores, lax.rem(place, cores)
    for j in range(quarters):
        for i in range(per_quarter):
            start = j * width + i * depth
            moved[start : start + depth, :] = x_ref[(dom ^ j) * per_quarter + i]
    for k in range(chips):
        for g in range(cores):
            at = (k * cores + g) * depth
            for j in range(quarters):
                if k == 0:
                    block = sources[g][0].at[dom ^ j]
                else:
                    block = sources[g][1 + order.index(k) * quarters + j]
                for i in range(width // lanes):
                    column = j * width + i * lanes
                    first[at : at + depth, column : column + lanes] = block[
                        i * depth : (i + 1) * depth, :
                    ]
                row = width // lanes * depth
                start = pl.multiple_of((dom ^ j) * width, lanes)
                second[pl.ds(start, width), at : at + depth] = block[row : row + width, :]
                row += width
                start = pl.multiple_of((dom ^ j) * chan, chan)
                env[pl.ds(start, chan), at : at + depth] = block[row : row + chan, :]
    value = jnp.dot(first[...], moved[...], preferred_element_type=f32)
    hidden[...] = (value / (1.0 + jnp.exp(-value))).astype(bf16)
    update = jnp.dot(second[...], hidden[...], preferred_element_type=f32)
    for s in range(shards):
        rows = slice(s * depth, (s + 1) * depth)
        fresh[s] = (x_ref[s].astype(f32) + update[rows, :]).astype(bf16)
    copies = [
        pltpu.make_async_copy(fresh.at[place ^ s], out, sems.at[s])
        for s, out in enumerate(new_refs)
    ]
    for copy in copies:
        copy.start()
    for k in range(chips):
        for g in range(cores):
            at = (k * cores + g) * depth
            source = (chip ^ k) * cores + (core if g == 0 else 1 - core)
            moved[at : at + depth, :] = fresh[source]
    rows = jnp.dot(env[...], moved[...], preferred_element_type=f32).astype(bf16)
    per = rows.shape[0] // shards
    for s in range(shards):
        rows_out[s] = rows[s * per : (s + 1) * per, :]
    copies.append(pltpu.make_async_copy(rows_out, out_ref, sems.at[shards]))
    copies[-1].start()
    for copy in copies:
        copy.wait()


def split_kernel(x_ref, tie_ref, out_ref, held, sems_in, sems_out):
    shards, _, edges = held.shape
    arriving = [
        pltpu.make_async_copy(x_ref.at[:, pl.ds(s * edges, edges)], held.at[s], sems_in.at[s])
        for s in range(shards)
    ]
    leaving = [
        pltpu.make_async_copy(held.at[s], out_ref.at[s], sems_out.at[s]) for s in range(shards)
    ]
    for copy in arriving:
        copy.start()
    for before, after in zip(arriving, leaving):
        before.wait()
        after.start()
    for copy in leaving:
        copy.wait()


def join_kernel(tie_ref, *refs):
    pieces, (out_ref, sems) = refs[:-2], refs[-2:]
    edges = pieces[0].shape[1]
    copies = []
    for s, piece in enumerate(pieces):
        at = pl.multiple_of((lax.axis_index("tp") ^ s) * edges, lanes)
        copies.append(pltpu.make_async_copy(piece, out_ref.at[:, pl.ds(at, edges)], sems.at[s]))
    for copy in copies:
        copy.start()
    for copy in copies:
        copy.wait()


def join_pieces(back, tie):
    depth, edges = back[0].shape
    return pl.pallas_call(
        join_kernel,
        out_shape=pltpu.HBM((depth, edges * len(back)), bf16),
        in_specs=[anywhere] + [in_vmem] * len(back),
        out_specs=in_hbm,
        scratch_shapes=[pltpu.SemaphoreType.DMA((len(back),))],
        compiler_params=grant(8),
        name="join",
    )(tie, *back)


def spread_mlp(latent, w_first, w_second, w_env, ties):
    domains = lax.axis_size("dom")
    shards = lax.axis_size("tp")
    chips = shards // cores
    total = w_first.shape[0]
    depth = w_first.shape[1]
    channels = w_env.shape[1]
    width = total // domains
    chan = channels // domains
    rows = 2 * width + chan
    edges = latent.shape[1] // shards
    full, own = pl.pallas_call(
        prepare_kernel,
        out_shape=(
            jax.ShapeDtypeStruct((domains, rows, depth), bf16),
            jax.ShapeDtypeStruct((rows, depth), bf16),
        ),
        in_specs=[in_hbm] * 3,
        out_specs=(in_vmem, in_vmem),
        scratch_shapes=[pltpu.VMEM(w.shape, bf16) for w in (w_first, w_second, w_env)]
        + [pltpu.SemaphoreType.DMA((3,))],
        compiler_params=grant(8),
        name="prepare",
    )(stay(w_first), stay(w_second), stay(w_env))
    pieces = pl.pallas_call(
        split_kernel,
        out_shape=pltpu.HBM((shards, depth, edges), bf16),
        in_specs=[in_hbm, anywhere],
        out_specs=in_hbm,
        scratch_shapes=[pltpu.VMEM((shards, depth, edges), bf16)]
        + [pltpu.SemaphoreType.DMA((shards,))] * 2,
        compiler_params=grant(8),
        name="split",
    )(stay(latent), own)
    order = hop_order(chips)
    shifted = {}
    for k in order:
        shifted[k] = flip_tp(own, k * cores)
    edge_rows = swap_blocks(pieces, "tp")
    edge_rows, *ties = lax.optimization_barrier((edge_rows, *ties))
    mine = [full]
    for k in order:
        mine += [shifted[k]] + [flip_dom(shifted[k], j) for j in range(1, domains)]
    others = [other_core(array) for array in mine]
    *new_rows, weight_rows = pl.pallas_call(
        functools.partial(mlp_kernel, quarters=domains, chips=chips, chan=chan, order=order),
        out_shape=[pltpu.HBM((depth, edges), bf16)] * shards
        + [pltpu.HBM((shards, channels // shards, edges), bf16)],
        in_specs=[in_vmem] * (1 + 2 * len(mine)),
        out_specs=[in_hbm] * (shards + 1),
        scratch_shapes=[
            pltpu.VMEM((total, total), bf16),
            pltpu.VMEM((total, total), bf16),
            pltpu.VMEM((channels, total), bf16),
            pltpu.VMEM((total, edges), bf16),
            pltpu.VMEM((total, edges), bf16),
            pltpu.VMEM((shards, depth, edges), bf16),
            pltpu.VMEM((shards, channels // shards, edges), bf16),
            pltpu.SemaphoreType.DMA((shards + 1,)),
        ],
        compiler_params=grant(28),
        name="mlp",
    )(edge_rows, *mine, *others)
    weights = swap_blocks(weight_rows, "tp")
    back = {0: new_rows[0]}
    for s in range(1, shards):
        back[s] = flip_tp(new_rows[s], s)
    back = [back[s] for s in range(shards)]
    return (lambda tie: join_pieces(back, tie)), weights, ties


def gathered_mlp(latent, w_first, w_second, w_env, ties):
    edge_rows = lax.all_to_all(latent, "tp", split_axis=1, concat_axis=0, tiled=True)
    full_first = lax.all_gather(w_first, "tp", axis=1, tiled=True)
    full_second = lax.all_gather(w_second, "tp", axis=0, tiled=True)
    full_env = lax.all_gather(w_env, "tp", axis=0, tiled=True)
    hidden = jax.nn.silu(contract_rows(full_first, edge_rows)).astype(bf16)
    update = contract_rows(full_second, hidden)
    new_rows = (edge_rows.astype(f32) + update).astype(bf16)
    weight_rows = contract_rows(full_env, new_rows).astype(bf16)
    shards = lax.axis_size("tp")
    weights = swap_blocks(weight_rows.reshape(shards, -1, weight_rows.shape[1]), "tp")
    new_rows, weights = lax.optimization_barrier((new_rows, weights))
    latent_new = lax.all_to_all(new_rows, "tp", split_axis=0, concat_axis=1, tiled=True)
    return (lambda tie: latent_new), weights, ties


def geometry_kernel(fill_ref, table_ref, vec_ref, centers_ref, species_ref, out_ref, gain_ref, rows):
    species_count, chan = table_ref.shape
    for b in range(centers_ref.shape[0]):
        rows[:, b, :] = vec_ref[:, b * lanes : (b + 1) * lanes]
        ids = lax.broadcasted_iota(jnp.int32, (1, lanes), 1)
        out_ref[parts, b : b + 1, :] = (ids < fill_ref[b]).astype(f32)
    alive = out_ref[parts]
    for m, part in enumerate(harmonics([rows[i] for i in range(3)])):
        out_ref[m] = part * alive
    out_ref[parts] = centers_ref[...].astype(f32)
    species = species_ref[...]
    for c in range(chan):
        gain = jnp.zeros(species.shape, f32)
        for kind in range(species_count):
            gain = jnp.where(species == kind, table_ref[kind, c], gain)
        gain_ref[c : c + 1, :] = gain


def select_atoms(h_ref, block, atoms):
    ids = lax.broadcasted_iota(jnp.int32, (atoms, lanes), 0).astype(f32)
    return (ids == h_ref[parts, pl.ds(block, 1), :]).astype(f32).astype(bf16)


def sums_kernel(dest_ref, w_ref, h_ref, *refs):
    outs, total = refs[:-1], refs[-1]
    shards, _, edges = w_ref.shape
    atoms = total.shape[2]
    per = edges // lanes
    total[...] = jnp.zeros_like(total)

    def step(s, carry):
        for i in range(per):
            block = s * per + i
            weight = w_ref[s, :, i * lanes : (i + 1) * lanes].astype(f32)
            terms = [
                (h_ref[m, pl.ds(block, 1), :] * weight).astype(bf16) for m in range(parts)
            ]
            contrib = jnp.concatenate(terms, axis=0)
            chosen = select_atoms(h_ref, block, atoms)
            slot = dest_ref[block] ^ lax.axis_index("dom")
            total[slot] += lax.dot_general(
                contrib, chosen, (((1,), (1,)), ((), ())), preferred_element_type=f32
            )
        return carry

    lax.fori_loop(0, shards, step, 0)
    for j, out in enumerate(outs):
        out[...] = total[j].astype(out.dtype)


def invariants_kernel(dest_ref, w_ref, h_ref, *refs):
    domains = len(refs) - 5
    result_ref, token_ref, env, out_ref, sems = refs[domains:]
    token_ref[...] = jnp.zeros_like(token_ref)
    shards, chan, edges = w_ref.shape
    atoms = env.shape[2]
    per = edges // lanes
    for j in range(domains):
        env[j] = refs[j][...]

    def step(s, carry):
        for i in range(per):
            block = s * per + i
            weight = w_ref[s, :, i * lanes : (i + 1) * lanes].astype(f32)
            chosen = select_atoms(h_ref, block, atoms)
            slot = dest_ref[block] ^ lax.axis_index("dom")
            found = jnp.dot(env[slot], chosen, preferred_element_type=f32)
            products = [
                found[m * chan : (m + 1) * chan, :] * h_ref[m, pl.ds(block, 1), :]
                for m in range(parts)
            ]
            at = pl.multiple_of(block * lanes, lanes)
            out_ref[0, :, pl.ds(at, lanes)] = products[0] * weight
            out_ref[1, :, pl.ds(at, lanes)] = sum(products[2:4], products[1]) * weight
            out_ref[2, :, pl.ds(at, lanes)] = sum(products[5:9], products[4]) * weight
        leave(s).start()
        return carry

    def leave(s):
        chunk = (slice(None), slice(None), pl.ds(pl.multiple_of(s * edges, lanes), edges))
        return pltpu.make_async_copy(out_ref.at[chunk], result_ref.at[chunk], sems.at[s])

    lax.fori_loop(0, shards, step, 0)
    for s in range(shards):
        leave(s).wait()


def on_device(
    latent,
    w_first,
    w_second,
    w_env,
    edge_vec,
    centers,
    block_dest,
    block_fill,
    species,
    species_gain,
):
    domains = lax.axis_size("dom")
    shards = lax.axis_size("tp")
    nblocks = block_fill.shape[0]
    atoms = species.shape[0]
    chan = species_gain.shape[1]
    depth, edges = latent.shape
    spread = (
        depth == lanes
        and w_first.shape[0] % (domains * lanes) == 0
        and w_env.shape[1] % (domains * 16) == 0
        and shards % cores == 0
        and shards & (shards - 1) == 0
        and domains & (domains - 1) == 0
    )
    harmonic, gain_sel = pl.pallas_call(
        geometry_kernel,
        out_shape=(
            jax.ShapeDtypeStruct((parts + 1, nblocks, lanes), f32),
            jax.ShapeDtypeStruct((chan, atoms), f32),
        ),
        in_specs=[in_smem] * 2 + [in_vmem] * 3,
        out_specs=(in_vmem, in_vmem),
        scratch_shapes=[pltpu.VMEM((3, nblocks, lanes), f32)],
        compiler_params=grant(4),
        name="geometry",
    )(
        stay(block_fill),
        stay(species_gain),
        edge_vec,
        centers.reshape(nblocks, lanes),
        species[None, :],
    )
    target = stay(block_dest[:, 0])
    mlp = spread_mlp if spread else gathered_mlp
    finish, weights, (harmonic, gain_sel) = mlp(
        latent, w_first, w_second, w_env, (harmonic, gain_sel)
    )

    rows = parts * chan
    sums = pl.pallas_call(
        sums_kernel,
        out_shape=[jax.ShapeDtypeStruct((rows, atoms), f32)]
        + [jax.ShapeDtypeStruct((rows, atoms), bf16)] * (domains - 1),
        in_specs=[in_smem] + [in_vmem] * 2,
        out_specs=[in_vmem] * domains,
        scratch_shapes=[pltpu.VMEM((domains, rows, atoms), f32)],
        compiler_params=grant(8),
        name="sums",
    )(target, weights, harmonic)
    env_raw = sums[0]
    for j in range(1, domains):
        arrived = flip_dom(sums[j], j)
        env_raw = env_raw + arrived.astype(f32)
    env_out = env_raw.reshape(parts, chan, atoms) * gain_sel[None, :, :] * env_factor
    env_half = env_out.astype(bf16).reshape(rows, atoms)
    looked = [env_half] + [flip_dom(env_half, j) for j in range(1, domains)]
    invariants, token = pl.pallas_call(
        invariants_kernel,
        out_shape=(
            pltpu.HBM((3, chan, edges), f32),
            jax.ShapeDtypeStruct((8, lanes), f32),
        ),
        in_specs=[in_smem] + [in_vmem] * (2 + domains),
        out_specs=(in_hbm, in_vmem),
        scratch_shapes=[
            pltpu.VMEM((domains, rows, atoms), bf16),
            pltpu.VMEM((3, chan, edges), f32),
            pltpu.SemaphoreType.DMA((shards,)),
        ],
        compiler_params=grant(10),
        name="invariants",
    )(target, weights, harmonic, *looked)
    return (finish(token), env_out, invariants)


def solution(mesh):
    in_specs = (
        P("tp", "dom"),
        P(None, "tp"),
        P("tp", None),
        P("tp", None),
        P(None, "dom"),
        P("dom"),
        P("dom", None),
        P("dom"),
        P("dom"),
        P(None, "tp"),
    )
    out_specs = (P("tp", "dom"), P(None, "tp", "dom"), P(None, "tp", "dom"))

    return jax.shard_map(on_device, mesh=mesh, in_specs=in_specs, out_specs=out_specs, check_vma=False)
```

```python
import functools
import math

import jax
import jax.numpy as jnp
from jax import lax
from jax.experimental import pallas as pl
from jax.experimental.pallas import tpu as pltpu
from jax.sharding import PartitionSpec as P


root_three = math.sqrt(3.0)
root_five = math.sqrt(5.0)
root_fifteen = math.sqrt(15.0)
cutoff_radius = 6.0
parts = 9
env_factor = 0.25
lanes = 128
cores = 2
bf16 = jnp.bfloat16
f32 = jnp.float32


mib = 1024 * 1024
in_vmem = pl.BlockSpec(memory_space=pltpu.VMEM)
in_smem = pl.BlockSpec(memory_space=pltpu.SMEM)
in_hbm = pl.BlockSpec(memory_space=pltpu.HBM)
anywhere = pl.BlockSpec(memory_space=pl.ANY)


def harmonics(vectors):
    along_x = vectors[0]
    along_y = vectors[1]
    along_z = vectors[2]
    radius = jnp.sqrt(along_x * along_x + along_y * along_y + along_z * along_z)
    unit_x = along_x / radius
    unit_y = along_y / radius
    unit_z = along_z / radius
    ratio = radius / cutoff_radius
    envelope = (1.0 - ratio * ratio) ** 2
    factors = [
        jnp.ones_like(unit_x),
        root_three * unit_x,
        root_three * unit_y,
        root_three * unit_z,
        root_fifteen * unit_x * unit_y,
        root_fifteen * unit_y * unit_z,
        root_five / 2.0 * (3.0 * unit_z * unit_z - 1.0),
        root_fifteen * unit_x * unit_z,
        root_fifteen / 2.0 * (unit_x * unit_x - unit_y * unit_y),
    ]
    return [factor * envelope for factor in factors]


def contract_rows(left, right):
    return lax.dot_general(
        left, right, (((0,), (0,)), ((), ())), preferred_element_type=f32
    )


def swap_blocks(array, axis):
    return lax.all_to_all(array, axis, split_axis=0, concat_axis=0, tiled=True)


def flip_dom(array, mask):
    count = lax.axis_size("dom")
    return lax.ppermute(array, "dom", [(i, i ^ mask) for i in range(count)])


def hop_order(chips):
    return sorted(range(1, chips), key=lambda k: (k.bit_length(), -k))


def flip_tp(array, mask):
    count = lax.axis_size("tp")
    return lax.ppermute(array, "tp", [(t, t ^ mask) for t in range(count)])


def other_core(array):
    return flip_tp(array, 1)


def stay(array):
    return pltpu.with_memory_space_constraint(array, pltpu.HBM)


def grant(size):
    return pltpu.CompilerParams(vmem_limit_bytes=size * mib)


def prepare_kernel(*refs):
    sources, (full_ref, own_ref), held, sems = refs[:3], refs[3:5], refs[5:8], refs[8]
    copies = [
        pltpu.make_async_copy(source, place, sems.at[i])
        for i, (source, place) in enumerate(zip(sources, held))
    ]
    for copy in copies:
        copy.start()
    first_ref, second_ref, env_ref = held
    quarters = full_ref.shape[0]
    width = first_ref.shape[0] // quarters
    chan = env_ref.shape[1] // quarters
    copies[0].wait()
    for q in range(quarters):
        for i in range(width // lanes):
            start = q * width + i * lanes
            full_ref[q, i * lanes : (i + 1) * lanes, :] = first_ref[start : start + lanes, :].T
    copies[1].wait()
    for q in range(quarters):
        full_ref[q, width : 2 * width, :] = second_ref[:, q * width : (q + 1) * width].T
    copies[2].wait()
    for q in range(quarters):
        full_ref[q, 2 * width :, :] = env_ref[:, q * chan : (q + 1) * chan].T
    own_ref[...] = full_ref[lax.axis_index("dom")]


def mlp_kernel(x_ref, *refs, quarters, chips, chan, order):
    per_group = 1 + len(order) * quarters
    sources = [refs[g * per_group : (g + 1) * per_group] for g in range(cores)]
    shards, depth, _ = x_ref.shape
    outs = refs[cores * per_group :]
    new_refs, outs = outs[:shards], outs[shards:]
    out_ref, first, second, env, moved, hidden, fresh, rows_out, sems = outs
    total = shards * depth
    width = total // quarters
    per_quarter = shards // quarters
    dom, place = lax.axis_index("dom"), lax.axis_index("tp")
    chip, core = place // cores, lax.rem(place, cores)
    for j in range(quarters):
        for i in range(per_quarter):
            start = j * width + i * depth
            moved[start : start + depth, :] = x_ref[(dom ^ j) * per_quarter + i]
    for k in range(chips):
        for g in range(cores):
            at = (k * cores + g) * depth
            for j in range(quarters):
                if k == 0:
                    block = sources[g][0].at[dom ^ j]
                else:
                    block = sources[g][1 + order.index(k) * quarters + j]
                for i in range(width // lanes):
                    column = j * width + i * lanes
                    first[at : at + depth, column : column + lanes] = block[
                        i * depth : (i + 1) * depth, :
                    ]
                row = width // lanes * depth
                start = pl.multiple_of((dom ^ j) * width, lanes)
                second[pl.ds(start, width), at : at + depth] = block[row : row + width, :]
                row += width
                start = pl.multiple_of((dom ^ j) * chan, chan)
                env[pl.ds(start, chan), at : at + depth] = block[row : row + chan, :]
    value = jnp.dot(first[...], moved[...], preferred_element_type=f32)
    hidden[...] = (value / (1.0 + jnp.exp(-value))).astype(bf16)
    update = jnp.dot(second[...], hidden[...], preferred_element_type=f32)
    for s in range(shards):
        rows = slice(s * depth, (s + 1) * depth)
        fresh[s] = (x_ref[s].astype(f32) + update[rows, :]).astype(bf16)
    copies = [
        pltpu.make_async_copy(fresh.at[place ^ s], out, sems.at[s])
        for s, out in enumerate(new_refs)
    ]
    for copy in copies:
        copy.start()
    for k in range(chips):
        for g in range(cores):
            at = (k * cores + g) * depth
            source = (chip ^ k) * cores + (core if g == 0 else 1 - core)
            moved[at : at + depth, :] = fresh[source]
    rows = jnp.dot(env[...], moved[...], preferred_element_type=f32).astype(bf16)
    per = rows.shape[0] // shards
    for s in range(shards):
        rows_out[s] = rows[s * per : (s + 1) * per, :]
    copies.append(pltpu.make_async_copy(rows_out, out_ref, sems.at[shards]))
    copies[-1].start()
    for copy in copies:
        copy.wait()


def split_kernel(x_ref, tie_ref, out_ref, held, sems_in, sems_out):
    shards, _, edges = held.shape
    arriving = [
        pltpu.make_async_copy(x_ref.at[:, pl.ds(s * edges, edges)], held.at[s], sems_in.at[s])
        for s in range(shards)
    ]
    leaving = [
        pltpu.make_async_copy(held.at[s], out_ref.at[s], sems_out.at[s]) for s in range(shards)
    ]
    for copy in arriving:
        copy.start()
    for before, after in zip(arriving, leaving):
        before.wait()
        after.start()
    for copy in leaving:
        copy.wait()


def join_kernel(tie_ref, *refs):
    pieces, (out_ref, sems) = refs[:-2], refs[-2:]
    edges = pieces[0].shape[1]
    copies = []
    for s, piece in enumerate(pieces):
        at = pl.multiple_of((lax.axis_index("tp") ^ s) * edges, lanes)
        copies.append(pltpu.make_async_copy(piece, out_ref.at[:, pl.ds(at, edges)], sems.at[s]))
    for copy in copies:
        copy.start()
    for copy in copies:
        copy.wait()


def join_pieces(back, tie):
    depth, edges = back[0].shape
    return pl.pallas_call(
        join_kernel,
        out_shape=pltpu.HBM((depth, edges * len(back)), bf16),
        in_specs=[anywhere] + [in_vmem] * len(back),
        out_specs=in_hbm,
        scratch_shapes=[pltpu.SemaphoreType.DMA((len(back),))],
        compiler_params=grant(8),
        name="join",
    )(tie, *back)


def spread_mlp(latent, w_first, w_second, w_env, ties):
    domains = lax.axis_size("dom")
    shards = lax.axis_size("tp")
    chips = shards // cores
    total = w_first.shape[0]
    depth = w_first.shape[1]
    channels = w_env.shape[1]
    width = total // domains
    chan = channels // domains
    rows = 2 * width + chan
    edges = latent.shape[1] // shards
    full, own = pl.pallas_call(
        prepare_kernel,
        out_shape=(
            jax.ShapeDtypeStruct((domains, rows, depth), bf16),
            jax.ShapeDtypeStruct((rows, depth), bf16),
        ),
        in_specs=[in_hbm] * 3,
        out_specs=(in_vmem, in_vmem),
        scratch_shapes=[pltpu.VMEM(w.shape, bf16) for w in (w_first, w_second, w_env)]
        + [pltpu.SemaphoreType.DMA((3,))],
        compiler_params=grant(8),
        name="prepare",
    )(stay(w_first), stay(w_second), stay(w_env))
    pieces = pl.pallas_call(
        split_kernel,
        out_shape=pltpu.HBM((shards, depth, edges), bf16),
        in_specs=[in_hbm, anywhere],
        out_specs=in_hbm,
        scratch_shapes=[pltpu.VMEM((shards, depth, edges), bf16)]
        + [pltpu.SemaphoreType.DMA((shards,))] * 2,
        compiler_params=grant(8),
        name="split",
    )(stay(latent), own)
    order = hop_order(chips)
    shifted = {}
    for k in order:
        shifted[k] = flip_tp(own, k * cores)
    edge_rows = swap_blocks(pieces, "tp")
    edge_rows, *ties = lax.optimization_barrier((edge_rows, *ties))
    mine = [full]
    for k in order:
        mine += [shifted[k]] + [flip_dom(shifted[k], j) for j in range(1, domains)]
    others = [other_core(array) for array in mine]
    *new_rows, weight_rows = pl.pallas_call(
        functools.partial(mlp_kernel, quarters=domains, chips=chips, chan=chan, order=order),
        out_shape=[pltpu.HBM((depth, edges), bf16)] * shards
        + [pltpu.HBM((shards, channels // shards, edges), bf16)],
        in_specs=[in_vmem] * (1 + 2 * len(mine)),
        out_specs=[in_hbm] * (shards + 1),
        scratch_shapes=[
            pltpu.VMEM((total, total), bf16),
            pltpu.VMEM((total, total), bf16),
            pltpu.VMEM((channels, total), bf16),
            pltpu.VMEM((total, edges), bf16),
            pltpu.VMEM((total, edges), bf16),
            pltpu.VMEM((shards, depth, edges), bf16),
            pltpu.VMEM((shards, channels // shards, edges), bf16),
            pltpu.SemaphoreType.DMA((shards + 1,)),
        ],
        compiler_params=grant(28),
        name="mlp",
    )(edge_rows, *mine, *others)
    weights = swap_blocks(weight_rows, "tp")
    back = {0: new_rows[0]}
    for s in range(1, shards):
        back[s] = flip_tp(new_rows[s], s)
    back = [back[s] for s in range(shards)]
    return (lambda tie: join_pieces(back, tie)), weights, ties


def gathered_mlp(latent, w_first, w_second, w_env, ties):
    edge_rows = lax.all_to_all(latent, "tp", split_axis=1, concat_axis=0, tiled=True)
    full_first = lax.all_gather(w_first, "tp", axis=1, tiled=True)
    full_second = lax.all_gather(w_second, "tp", axis=0, tiled=True)
    full_env = lax.all_gather(w_env, "tp", axis=0, tiled=True)
    hidden = jax.nn.silu(contract_rows(full_first, edge_rows)).astype(bf16)
    update = contract_rows(full_second, hidden)
    new_rows = (edge_rows.astype(f32) + update).astype(bf16)
    weight_rows = contract_rows(full_env, new_rows).astype(bf16)
    shards = lax.axis_size("tp")
    weights = swap_blocks(weight_rows.reshape(shards, -1, weight_rows.shape[1]), "tp")
    new_rows, weights = lax.optimization_barrier((new_rows, weights))
    latent_new = lax.all_to_all(new_rows, "tp", split_axis=0, concat_axis=1, tiled=True)
    return (lambda tie: latent_new), weights, ties


def geometry_kernel(fill_ref, table_ref, vec_ref, centers_ref, species_ref, out_ref, gain_ref, rows):
    species_count, chan = table_ref.shape
    for b in range(centers_ref.shape[0]):
        rows[:, b, :] = vec_ref[:, b * lanes : (b + 1) * lanes]
        ids = lax.broadcasted_iota(jnp.int32, (1, lanes), 1)
        out_ref[parts, b : b + 1, :] = (ids < fill_ref[b]).astype(f32)
    alive = out_ref[parts]
    for m, part in enumerate(harmonics([rows[i] for i in range(3)])):
        out_ref[m] = part * alive
    out_ref[parts] = centers_ref[...].astype(f32)
    species = species_ref[...]
    for c in range(chan):
        gain = jnp.zeros(species.shape, f32)
        for kind in range(species_count):
            gain = jnp.where(species == kind, table_ref[kind, c], gain)
        gain_ref[c : c + 1, :] = gain


def select_atoms(h_ref, block, atoms):
    ids = lax.broadcasted_iota(jnp.int32, (atoms, lanes), 0).astype(f32)
    return (ids == h_ref[parts, pl.ds(block, 1), :]).astype(f32).astype(bf16)


def sums_kernel(dest_ref, w_ref, h_ref, *refs):
    outs, total = refs[:-1], refs[-1]
    shards, _, edges = w_ref.shape
    atoms = total.shape[2]
    per = edges // lanes
    total[...] = jnp.zeros_like(total)

    def step(s):
        for i in range(per):
            block = s * per + i
            weight = w_ref[s, :, i * lanes : (i + 1) * lanes].astype(f32)
            terms = [
                (h_ref[m, pl.ds(block, 1), :] * weight).astype(bf16) for m in range(parts)
            ]
            contrib = jnp.concatenate(terms, axis=0)
            chosen = select_atoms(h_ref, block, atoms)
            slot = dest_ref[block] ^ lax.axis_index("dom")
            total[slot] += lax.dot_general(
                contrib, chosen, (((1,), (1,)), ((), ())), preferred_element_type=f32
            )

    for s in range(shards):
        step(s)
    for j, out in enumerate(outs):
        out[...] = total[j].astype(out.dtype)


def invariants_kernel(dest_ref, w_ref, h_ref, *refs):
    domains = len(refs) - 5
    result_ref, token_ref, env, out_ref, sems = refs[domains:]
    token_ref[...] = jnp.zeros_like(token_ref)
    shards, chan, edges = w_ref.shape
    atoms = env.shape[2]
    per = edges // lanes
    for j in range(domains):
        env[j] = refs[j][...]

    def step(s):
        for i in range(per):
            block = s * per + i
            weight = w_ref[s, :, i * lanes : (i + 1) * lanes].astype(f32)
            chosen = select_atoms(h_ref, block, atoms)
            slot = dest_ref[block] ^ lax.axis_index("dom")
            found = jnp.dot(env[slot], chosen, preferred_element_type=f32)
            products = [
                found[m * chan : (m + 1) * chan, :] * h_ref[m, pl.ds(block, 1), :]
                for m in range(parts)
            ]
            at = block * lanes
            out_ref[0, :, pl.ds(at, lanes)] = products[0] * weight
            out_ref[1, :, pl.ds(at, lanes)] = sum(products[2:4], products[1]) * weight
            out_ref[2, :, pl.ds(at, lanes)] = sum(products[5:9], products[4]) * weight
        leave(s).start()

    def leave(s):
        chunk = (slice(None), slice(None), pl.ds(s * edges, edges))
        return pltpu.make_async_copy(out_ref.at[chunk], result_ref.at[chunk], sems.at[s])

    for s in range(shards):
        step(s)
    for s in range(shards):
        leave(s).wait()


def on_device(
    latent,
    w_first,
    w_second,
    w_env,
    edge_vec,
    centers,
    block_dest,
    block_fill,
    species,
    species_gain,
):
    domains = lax.axis_size("dom")
    shards = lax.axis_size("tp")
    nblocks = block_fill.shape[0]
    atoms = species.shape[0]
    chan = species_gain.shape[1]
    depth, edges = latent.shape
    spread = (
        depth == lanes
        and w_first.shape[0] % (domains * lanes) == 0
        and w_env.shape[1] % (domains * 16) == 0
        and shards % cores == 0
        and shards & (shards - 1) == 0
        and domains & (domains - 1) == 0
    )
    harmonic, gain_sel = pl.pallas_call(
        geometry_kernel,
        out_shape=(
            jax.ShapeDtypeStruct((parts + 1, nblocks, lanes), f32),
            jax.ShapeDtypeStruct((chan, atoms), f32),
        ),
        in_specs=[in_smem] * 2 + [in_vmem] * 3,
        out_specs=(in_vmem, in_vmem),
        scratch_shapes=[pltpu.VMEM((3, nblocks, lanes), f32)],
        compiler_params=grant(4),
        name="geometry",
    )(
        stay(block_fill),
        stay(species_gain),
        edge_vec,
        centers.reshape(nblocks, lanes),
        species[None, :],
    )
    target = stay(block_dest[:, 0])
    mlp = spread_mlp if spread else gathered_mlp
    finish, weights, (harmonic, gain_sel) = mlp(
        latent, w_first, w_second, w_env, (harmonic, gain_sel)
    )

    rows = parts * chan
    sums = pl.pallas_call(
        sums_kernel,
        out_shape=[jax.ShapeDtypeStruct((rows, atoms), f32)]
        + [jax.ShapeDtypeStruct((rows, atoms), bf16)] * (domains - 1),
        in_specs=[in_smem] + [in_vmem] * 2,
        out_specs=[in_vmem] * domains,
        scratch_shapes=[pltpu.VMEM((domains, rows, atoms), f32)],
        compiler_params=grant(8),
        name="sums",
    )(target, weights, harmonic)
    env_raw = sums[0]
    for j in range(1, domains):
        env_raw = env_raw + flip_dom(sums[j], j).astype(f32)
    env_out = env_raw.reshape(parts, chan, atoms) * gain_sel[None, :, :] * env_factor
    env_half = env_out.astype(bf16).reshape(rows, atoms)
    looked = [env_half] + [flip_dom(env_half, j) for j in range(1, domains)]
    invariants, token = pl.pallas_call(
        invariants_kernel,
        out_shape=(
            pltpu.HBM((3, chan, edges), f32),
            jax.ShapeDtypeStruct((8, lanes), f32),
        ),
        in_specs=[in_smem] + [in_vmem] * (2 + domains),
        out_specs=(in_hbm, in_vmem),
        scratch_shapes=[
            pltpu.VMEM((domains, rows, atoms), bf16),
            pltpu.VMEM((3, chan, edges), f32),
            pltpu.SemaphoreType.DMA((shards,)),
        ],
        compiler_params=grant(10),
        name="invariants",
    )(target, weights, harmonic, *looked)
    return (finish(token), env_out, invariants)


def solution(mesh):
    in_specs = (
        P("tp", "dom"),
        P(None, "tp"),
        P("tp", None),
        P("tp", None),
        P(None, "dom"),
        P("dom"),
        P("dom", None),
        P("dom"),
        P("dom"),
        P(None, "tp"),
    )
    out_specs = (P("tp", "dom"), P(None, "tp", "dom"), P(None, "tp", "dom"))

    return jax.shard_map(on_device, mesh=mesh, in_specs=in_specs, out_specs=out_specs, check_vma=False)
```

```python
import functools
import math

import jax
import jax.numpy as jnp
from jax import lax
from jax.experimental import pallas as pl
from jax.experimental.pallas import tpu as pltpu
from jax.sharding import PartitionSpec as P


root_three = math.sqrt(3.0)
root_five = math.sqrt(5.0)
root_fifteen = math.sqrt(15.0)
cutoff_radius = 6.0
parts = 9
env_factor = 0.25
lanes = 128
cores = 2
bf16 = jnp.bfloat16
f32 = jnp.float32


mib = 1024 * 1024
in_vmem = pl.BlockSpec(memory_space=pltpu.VMEM)
in_smem = pl.BlockSpec(memory_space=pltpu.SMEM)
in_hbm = pl.BlockSpec(memory_space=pltpu.HBM)
anywhere = pl.BlockSpec(memory_space=pl.ANY)


def harmonics(vectors):
    along_x = vectors[0]
    along_y = vectors[1]
    along_z = vectors[2]
    radius = jnp.sqrt(along_x * along_x + along_y * along_y + along_z * along_z)
    unit_x = along_x / radius
    unit_y = along_y / radius
    unit_z = along_z / radius
    ratio = radius / cutoff_radius
    envelope = (1.0 - ratio * ratio) ** 2
    factors = [
        jnp.ones_like(unit_x),
        root_three * unit_x,
        root_three * unit_y,
        root_three * unit_z,
        root_fifteen * unit_x * unit_y,
        root_fifteen * unit_y * unit_z,
        root_five / 2.0 * (3.0 * unit_z * unit_z - 1.0),
        root_fifteen * unit_x * unit_z,
        root_fifteen / 2.0 * (unit_x * unit_x - unit_y * unit_y),
    ]
    return [factor * envelope for factor in factors]


def contract_rows(left, right):
    return lax.dot_general(
        left, right, (((0,), (0,)), ((), ())), preferred_element_type=f32
    )


def swap_blocks(array, axis):
    return lax.all_to_all(array, axis, split_axis=0, concat_axis=0, tiled=True)


def flip_dom(array, mask):
    count = lax.axis_size("dom")
    return lax.ppermute(array, "dom", [(i, i ^ mask) for i in range(count)])


def hop_order(chips):
    return sorted(range(1, chips), key=lambda k: (k.bit_length(), -k))


def flip_tp(array, mask):
    count = lax.axis_size("tp")
    return lax.ppermute(array, "tp", [(t, t ^ mask) for t in range(count)])


def other_core(array):
    return flip_tp(array, 1)


def stay(array):
    return pltpu.with_memory_space_constraint(array, pltpu.HBM)


def grant(size):
    return pltpu.CompilerParams(vmem_limit_bytes=size * mib)


def prepare_kernel(*refs):
    sources, (full_ref, own_ref), held, sems = refs[:3], refs[3:5], refs[5:8], refs[8]
    copies = [
        pltpu.make_async_copy(source, place, sems.at[i])
        for i, (source, place) in enumerate(zip(sources, held))
    ]
    for copy in copies:
        copy.start()
    first_ref, second_ref, env_ref = held
    quarters = full_ref.shape[0]
    width = first_ref.shape[0] // quarters
    chan = env_ref.shape[1] // quarters
    copies[0].wait()
    for q in range(quarters):
        for i in range(width // lanes):
            start = q * width + i * lanes
            full_ref[q, i * lanes : (i + 1) * lanes, :] = first_ref[start : start + lanes, :].T
    copies[1].wait()
    for q in range(quarters):
        full_ref[q, width : 2 * width, :] = second_ref[:, q * width : (q + 1) * width].T
    copies[2].wait()
    for q in range(quarters):
        full_ref[q, 2 * width :, :] = env_ref[:, q * chan : (q + 1) * chan].T
    own_ref[...] = full_ref[lax.axis_index("dom")]


def mlp_kernel(x_ref, *refs, quarters, chips, chan, order):
    per_group = 1 + len(order) * quarters
    sources = [refs[g * per_group : (g + 1) * per_group] for g in range(cores)]
    shards, depth, _ = x_ref.shape
    outs = refs[cores * per_group :]
    new_refs, outs = outs[:shards], outs[shards:]
    out_ref, first, second, env, moved, hidden, fresh, rows_out, sems = outs
    total = shards * depth
    width = total // quarters
    per_quarter = shards // quarters
    dom, place = lax.axis_index("dom"), lax.axis_index("tp")
    chip, core = place // cores, lax.rem(place, cores)
    for j in range(quarters):
        for i in range(per_quarter):
            start = j * width + i * depth
            moved[start : start + depth, :] = x_ref[(dom ^ j) * per_quarter + i]
    for k in range(chips):
        for g in range(cores):
            at = (k * cores + g) * depth
            for j in range(quarters):
                if k == 0:
                    block = sources[g][0].at[dom ^ j]
                else:
                    block = sources[g][1 + order.index(k) * quarters + j]
                for i in range(width // lanes):
                    column = j * width + i * lanes
                    first[at : at + depth, column : column + lanes] = block[
                        i * depth : (i + 1) * depth, :
                    ]
                row = width // lanes * depth
                start = pl.multiple_of((dom ^ j) * width, lanes)
                second[pl.ds(start, width), at : at + depth] = block[row : row + width, :]
                row += width
                start = pl.multiple_of((dom ^ j) * chan, chan)
                env[pl.ds(start, chan), at : at + depth] = block[row : row + chan, :]
    for s in range(shards):
        rows = slice(s * depth, (s + 1) * depth)
        value = jnp.dot(first[rows, :], moved[...], preferred_element_type=f32)
        hidden[rows, :] = (value / (1.0 + jnp.exp(-value))).astype(bf16)
    for s in range(shards):
        rows = slice(s * depth, (s + 1) * depth)
        update = jnp.dot(second[rows, :], hidden[...], preferred_element_type=f32)
        fresh[s] = (x_ref[s].astype(f32) + update).astype(bf16)
    copies = [
        pltpu.make_async_copy(fresh.at[place ^ s], out, sems.at[s])
        for s, out in enumerate(new_refs)
    ]
    for copy in copies:
        copy.start()
    for k in range(chips):
        for g in range(cores):
            at = (k * cores + g) * depth
            source = (chip ^ k) * cores + (core if g == 0 else 1 - core)
            moved[at : at + depth, :] = fresh[source]
    rows = jnp.dot(env[...], moved[...], preferred_element_type=f32).astype(bf16)
    per = rows.shape[0] // shards
    for s in range(shards):
        rows_out[s] = rows[s * per : (s + 1) * per, :]
    copies.append(pltpu.make_async_copy(rows_out, out_ref, sems.at[shards]))
    copies[-1].start()
    for copy in copies:
        copy.wait()


def split_kernel(x_ref, tie_ref, out_ref, held, sems_in, sems_out):
    shards, _, edges = held.shape
    arriving = [
        pltpu.make_async_copy(x_ref.at[:, pl.ds(s * edges, edges)], held.at[s], sems_in.at[s])
        for s in range(shards)
    ]
    leaving = [
        pltpu.make_async_copy(held.at[s], out_ref.at[s], sems_out.at[s]) for s in range(shards)
    ]
    for copy in arriving:
        copy.start()
    for before, after in zip(arriving, leaving):
        before.wait()
        after.start()
    for copy in leaving:
        copy.wait()


def join_kernel(tie_ref, *refs):
    pieces, (out_ref, sems) = refs[:-2], refs[-2:]
    edges = pieces[0].shape[1]
    copies = []
    for s, piece in enumerate(pieces):
        at = pl.multiple_of((lax.axis_index("tp") ^ s) * edges, lanes)
        copies.append(pltpu.make_async_copy(piece, out_ref.at[:, pl.ds(at, edges)], sems.at[s]))
    for copy in copies:
        copy.start()
    for copy in copies:
        copy.wait()


def join_pieces(back, tie):
    depth, edges = back[0].shape
    return pl.pallas_call(
        join_kernel,
        out_shape=pltpu.HBM((depth, edges * len(back)), bf16),
        in_specs=[anywhere] + [in_vmem] * len(back),
        out_specs=in_hbm,
        scratch_shapes=[pltpu.SemaphoreType.DMA((len(back),))],
        compiler_params=grant(8),
        name="join",
    )(tie, *back)


def spread_mlp(latent, w_first, w_second, w_env, ties):
    domains = lax.axis_size("dom")
    shards = lax.axis_size("tp")
    chips = shards // cores
    total = w_first.shape[0]
    depth = w_first.shape[1]
    channels = w_env.shape[1]
    width = total // domains
    chan = channels // domains
    rows = 2 * width + chan
    edges = latent.shape[1] // shards
    full, own = pl.pallas_call(
        prepare_kernel,
        out_shape=(
            jax.ShapeDtypeStruct((domains, rows, depth), bf16),
            jax.ShapeDtypeStruct((rows, depth), bf16),
        ),
        in_specs=[in_hbm] * 3,
        out_specs=(in_vmem, in_vmem),
        scratch_shapes=[pltpu.VMEM(w.shape, bf16) for w in (w_first, w_second, w_env)]
        + [pltpu.SemaphoreType.DMA((3,))],
        compiler_params=grant(8),
        name="prepare",
    )(stay(w_first), stay(w_second), stay(w_env))
    pieces = pl.pallas_call(
        split_kernel,
        out_shape=pltpu.HBM((shards, depth, edges), bf16),
        in_specs=[in_hbm, anywhere],
        out_specs=in_hbm,
        scratch_shapes=[pltpu.VMEM((shards, depth, edges), bf16)]
        + [pltpu.SemaphoreType.DMA((shards,))] * 2,
        compiler_params=grant(8),
        name="split",
    )(stay(latent), own)
    order = hop_order(chips)
    shifted = {}
    for k in order:
        shifted[k] = flip_tp(own, k * cores)
    edge_rows = swap_blocks(pieces, "tp")
    edge_rows, *ties = lax.optimization_barrier((edge_rows, *ties))
    mine = [full]
    for k in order:
        mine += [shifted[k]] + [flip_dom(shifted[k], j) for j in range(1, domains)]
    others = [other_core(array) for array in mine]
    *new_rows, weight_rows = pl.pallas_call(
        functools.partial(mlp_kernel, quarters=domains, chips=chips, chan=chan, order=order),
        out_shape=[pltpu.HBM((depth, edges), bf16)] * shards
        + [pltpu.HBM((shards, channels // shards, edges), bf16)],
        in_specs=[in_vmem] * (1 + 2 * len(mine)),
        out_specs=[in_hbm] * (shards + 1),
        scratch_shapes=[
            pltpu.VMEM((total, total), bf16),
            pltpu.VMEM((total, total), bf16),
            pltpu.VMEM((channels, total), bf16),
            pltpu.VMEM((total, edges), bf16),
            pltpu.VMEM((total, edges), bf16),
            pltpu.VMEM((shards, depth, edges), bf16),
            pltpu.VMEM((shards, channels // shards, edges), bf16),
            pltpu.SemaphoreType.DMA((shards + 1,)),
        ],
        compiler_params=grant(28),
        name="mlp",
    )(edge_rows, *mine, *others)
    weights = swap_blocks(weight_rows, "tp")
    back = {0: new_rows[0]}
    for s in range(1, shards):
        back[s] = flip_tp(new_rows[s], s)
    back = [back[s] for s in range(shards)]
    return (lambda tie: join_pieces(back, tie)), weights, ties


def gathered_mlp(latent, w_first, w_second, w_env, ties):
    edge_rows = lax.all_to_all(latent, "tp", split_axis=1, concat_axis=0, tiled=True)
    full_first = lax.all_gather(w_first, "tp", axis=1, tiled=True)
    full_second = lax.all_gather(w_second, "tp", axis=0, tiled=True)
    full_env = lax.all_gather(w_env, "tp", axis=0, tiled=True)
    hidden = jax.nn.silu(contract_rows(full_first, edge_rows)).astype(bf16)
    update = contract_rows(full_second, hidden)
    new_rows = (edge_rows.astype(f32) + update).astype(bf16)
    weight_rows = contract_rows(full_env, new_rows).astype(bf16)
    shards = lax.axis_size("tp")
    weights = swap_blocks(weight_rows.reshape(shards, -1, weight_rows.shape[1]), "tp")
    new_rows, weights = lax.optimization_barrier((new_rows, weights))
    latent_new = lax.all_to_all(new_rows, "tp", split_axis=0, concat_axis=1, tiled=True)
    return (lambda tie: latent_new), weights, ties


def geometry_kernel(fill_ref, table_ref, vec_ref, centers_ref, species_ref, out_ref, gain_ref, rows):
    species_count, chan = table_ref.shape
    for b in range(centers_ref.shape[0]):
        rows[:, b, :] = vec_ref[:, b * lanes : (b + 1) * lanes]
        ids = lax.broadcasted_iota(jnp.int32, (1, lanes), 1)
        out_ref[parts, b : b + 1, :] = (ids < fill_ref[b]).astype(f32)
    alive = out_ref[parts]
    for m, part in enumerate(harmonics([rows[i] for i in range(3)])):
        out_ref[m] = part * alive
    out_ref[parts] = centers_ref[...].astype(f32)
    species = species_ref[...]
    for c in range(chan):
        gain = jnp.zeros(species.shape, f32)
        for kind in range(species_count):
            gain = jnp.where(species == kind, table_ref[kind, c], gain)
        gain_ref[c : c + 1, :] = gain


def select_atoms(h_ref, block, atoms):
    ids = lax.broadcasted_iota(jnp.int32, (atoms, lanes), 0).astype(f32)
    return (ids == h_ref[parts, pl.ds(block, 1), :]).astype(f32).astype(bf16)


def sums_kernel(dest_ref, w_ref, h_ref, *refs):
    outs, total = refs[:-1], refs[-1]
    shards, _, edges = w_ref.shape
    atoms = total.shape[2]
    per = edges // lanes
    total[...] = jnp.zeros_like(total)

    def step(s):
        for i in range(per):
            block = s * per + i
            weight = w_ref[s, :, i * lanes : (i + 1) * lanes].astype(f32)
            terms = [
                (h_ref[m, pl.ds(block, 1), :] * weight).astype(bf16) for m in range(parts)
            ]
            contrib = jnp.concatenate(terms, axis=0)
            chosen = select_atoms(h_ref, block, atoms)
            slot = dest_ref[block] ^ lax.axis_index("dom")
            total[slot] += lax.dot_general(
                contrib, chosen, (((1,), (1,)), ((), ())), preferred_element_type=f32
            )

    for s in range(shards):
        step(s)
    for j, out in enumerate(outs):
        out[...] = total[j].astype(out.dtype)


def invariants_kernel(dest_ref, w_ref, h_ref, *refs):
    domains = len(refs) - 5
    result_ref, token_ref, env, out_ref, sems = refs[domains:]
    token_ref[...] = jnp.zeros_like(token_ref)
    shards, chan, edges = w_ref.shape
    atoms = env.shape[2]
    per = edges // lanes
    for j in range(domains):
        env[j] = refs[j][...]

    def step(s):
        for i in range(per):
            block = s * per + i
            weight = w_ref[s, :, i * lanes : (i + 1) * lanes].astype(f32)
            chosen = select_atoms(h_ref, block, atoms)
            slot = dest_ref[block] ^ lax.axis_index("dom")
            found = jnp.dot(env[slot], chosen, preferred_element_type=f32)
            products = [
                found[m * chan : (m + 1) * chan, :] * h_ref[m, pl.ds(block, 1), :]
                for m in range(parts)
            ]
            at = block * lanes
            out_ref[0, :, pl.ds(at, lanes)] = products[0] * weight
            out_ref[1, :, pl.ds(at, lanes)] = sum(products[2:4], products[1]) * weight
            out_ref[2, :, pl.ds(at, lanes)] = sum(products[5:9], products[4]) * weight
        leave(s).start()

    def leave(s):
        chunk = (slice(None), slice(None), pl.ds(s * edges, edges))
        return pltpu.make_async_copy(out_ref.at[chunk], result_ref.at[chunk], sems.at[s])

    for s in range(shards):
        step(s)
    for s in range(shards):
        leave(s).wait()


def on_device(
    latent,
    w_first,
    w_second,
    w_env,
    edge_vec,
    centers,
    block_dest,
    block_fill,
    species,
    species_gain,
):
    domains = lax.axis_size("dom")
    shards = lax.axis_size("tp")
    nblocks = block_fill.shape[0]
    atoms = species.shape[0]
    chan = species_gain.shape[1]
    depth, edges = latent.shape
    spread = (
        depth == lanes
        and w_first.shape[0] % (domains * lanes) == 0
        and w_env.shape[1] % (domains * 16) == 0
        and shards % cores == 0
        and shards & (shards - 1) == 0
        and domains & (domains - 1) == 0
    )
    harmonic, gain_sel = pl.pallas_call(
        geometry_kernel,
        out_shape=(
            jax.ShapeDtypeStruct((parts + 1, nblocks, lanes), f32),
            jax.ShapeDtypeStruct((chan, atoms), f32),
        ),
        in_specs=[in_smem] * 2 + [in_vmem] * 3,
        out_specs=(in_vmem, in_vmem),
        scratch_shapes=[pltpu.VMEM((3, nblocks, lanes), f32)],
        compiler_params=grant(4),
        name="geometry",
    )(
        stay(block_fill),
        stay(species_gain),
        edge_vec,
        centers.reshape(nblocks, lanes),
        species[None, :],
    )
    target = stay(block_dest[:, 0])
    mlp = spread_mlp if spread else gathered_mlp
    finish, weights, (harmonic, gain_sel) = mlp(
        latent, w_first, w_second, w_env, (harmonic, gain_sel)
    )

    rows = parts * chan
    sums = pl.pallas_call(
        sums_kernel,
        out_shape=[jax.ShapeDtypeStruct((rows, atoms), f32)]
        + [jax.ShapeDtypeStruct((rows, atoms), bf16)] * (domains - 1),
        in_specs=[in_smem] + [in_vmem] * 2,
        out_specs=[in_vmem] * domains,
        scratch_shapes=[pltpu.VMEM((domains, rows, atoms), f32)],
        compiler_params=grant(8),
        name="sums",
    )(target, weights, harmonic)
    env_raw = sums[0]
    for j in range(1, domains):
        env_raw = env_raw + flip_dom(sums[j], j).astype(f32)
    env_out = env_raw.reshape(parts, chan, atoms) * gain_sel[None, :, :] * env_factor
    env_half = env_out.astype(bf16).reshape(rows, atoms)
    looked = [env_half] + [flip_dom(env_half, j) for j in range(1, domains)]
    invariants, token = pl.pallas_call(
        invariants_kernel,
        out_shape=(
            pltpu.HBM((3, chan, edges), f32),
            jax.ShapeDtypeStruct((8, lanes), f32),
        ),
        in_specs=[in_smem] + [in_vmem] * (2 + domains),
        out_specs=(in_hbm, in_vmem),
        scratch_shapes=[
            pltpu.VMEM((domains, rows, atoms), bf16),
            pltpu.VMEM((3, chan, edges), f32),
            pltpu.SemaphoreType.DMA((shards,)),
        ],
        compiler_params=grant(10),
        name="invariants",
    )(target, weights, harmonic, *looked)
    return (finish(token), env_out, invariants)


def solution(mesh):
    in_specs = (
        P("tp", "dom"),
        P(None, "tp"),
        P("tp", None),
        P("tp", None),
        P(None, "dom"),
        P("dom"),
        P("dom", None),
        P("dom"),
        P("dom"),
        P(None, "tp"),
    )
    out_specs = (P("tp", "dom"), P(None, "tp", "dom"), P(None, "tp", "dom"))

    return jax.shard_map(on_device, mesh=mesh, in_specs=in_specs, out_specs=out_specs, check_vma=False)
```
